256 devices in a mesh: gx: 32 (over x, z), gy: 4 (over y), gz: 2 (over core).
Axes of the slice: x: 4, y: 4, z: 8, core: 2. Of those that a mesh axis runs over, the one named last changes fastest.
Arguments:
- offsets: float32 [3, 32, 8, 16, 128], P(None, 'gx', 'gy', 'gz'), may hold values from 0 to 1
- counts: int32 [32, 8, 16], P('gx', 'gy', 'gz'), may hold values from 32 to 128
- correction: float32 [32, 8, 16, 128], P('gx', 'gy', 'gz'), may hold values from 0.25 to 1.75
- dirichlet: float32 [32, 8, 16, 128], P('gx', 'gy', 'gz'), may hold values from 0.05 to 1
- right_side: float32 [32, 8, 16, 128], P('gx', 'gy', 'gz'), may hold values from -15 to 15
- deflation: float32 [64, 32, 8, 16, 128], P(None, 'gx', 'gy', 'gz'), may hold values from -0.5 to 0.5
- coarse_inverse: float32 [16384, 16384], P(('gx', 'gy', 'gz')), may hold values from -1 to 2.5, as said below
Outputs:
- pressure: float32 [32, 8, 16, 128], P('gx', 'gy', 'gz')
- residual: float32 [32, 8, 16, 128], P('gx', 'gy', 'gz')
- direction: float32 [32, 8, 16, 128], P('gx', 'gy', 'gz')
The draws below stay inside these ranges and needn't reach their ends.
Inputs may be any that keep to these rules, and one draw needn't show every extreme that they name: coarse_inverse is symmetric and positive definite.
All inputs are finite; a program needn't handle non-finite values.
Results may differ from the reference program's by a relative error of at most 0.0003.
Values sent between devices are 32-bit elements; how exact they have to be, the bound alone decides.
No kernel may reach another device: no remote copies, remote signals or barrier semaphores. Data moves between devices by JAX's collectives and lax.ppermute only.
A program may use at most 64 MiB of HBM per device.

```python
import math
import jax
import jax.numpy as jnp
from jax import lax

CX = 1
CY = 2
CZ = 8
SLOTS = 128
NDEF = 64
ITERS = 2
NX = 32
NY = 8
NZ = 16
COARSE = 16384
N_GX = 32
N_GY = 4
N_GZ = 2


def draw_right_side(key, part):
    growth = 1.0 + 2.0 * jnp.arange(NX, dtype=jnp.float32) / max(NX - 1, 1)
    scaling = growth[:, None, None, None]
    sample_base = jnp.clip(jax.random.normal(key, (NX, NY, NZ, SLOTS), jnp.float32), -5.0, 5.0)
    return scaling * sample_base


def draw_coarse_inverse(key, part):
    key_diag, key_off = jax.random.split(jax.random.fold_in(key, 17))
    matrix_order = COARSE
    pieces = jax.random.normal(key_off, (matrix_order, matrix_order), jnp.float32) * (0.3 / math.sqrt(2.0 * matrix_order))
    symmetric = pieces + pieces.T
    diagonal = jax.random.uniform(key_diag, (matrix_order,), jnp.float32, 1.0, 2.0)
    return symmetric + jnp.diag(diagonal)


def touch_ends(drawn, rng, low, top_value):
    dims = drawn.shape
    place = [jax.random.randint(jax.random.fold_in(rng, axis), (), 0, dims[axis]) for axis in range(len(dims))]
    drawn = drawn.at[tuple(place)].set(low)
    longest = dims.index(max(dims))
    place[longest] = (place[longest] + 1) % dims[longest]
    return drawn.at[tuple(place)].set(top_value)


def shard_levels(rng, dims, cuts, least, top_value):
    def one(axis_at, shards_of):
        heights = jax.random.uniform(jax.random.fold_in(jax.random.fold_in(rng, 6), axis_at), (shards_of,), jnp.float32, least / len(cuts), top_value / len(cuts))
        return jnp.repeat(jnp.exp(heights), dims[axis_at] // shards_of).reshape((-1,) + (1,) * (len(dims) - axis_at - 1))

    level = one(*cuts[0])
    for cut in cuts[1:]:
        level = level * one(*cut)
    return level


def bell_draw(key, shape, width, bound, cuts=(), kind=jnp.bfloat16):
    values = width * jax.random.normal(key, shape, jnp.float32)
    if cuts:
        values = values * shard_levels(key, shape, cuts, -0.22, 0.18)
    return jnp.clip(values, -bound, bound).astype(kind)


def setup_inputs(seed: int = 0) -> dict:
    streams_of = jax.random.split(jax.random.key(seed), 8)
    return {
        "offsets": jnp.clip(1.0 * jax.random.uniform(streams_of[0], (3, NX, NY, NZ, SLOTS), jnp.float32) ** shard_levels(streams_of[0], (3, NX, NY, NZ, SLOTS), ((1, 32), (2, 4), (3, 2)), -0.2, 0.2), 0.0, 1.0),
        "counts": touch_ends(jax.random.randint(streams_of[1], (NX, NY, NZ), SLOTS // 4, SLOTS + 1), jax.random.fold_in(streams_of[1], 1), SLOTS // 4, SLOTS).astype(jnp.int32),
        "correction": jnp.clip(1.0 + 0.15 * jax.random.normal(streams_of[2], (NX, NY, NZ, SLOTS), jnp.float32), 0.25, 1.75),
        "dirichlet": jnp.clip(jnp.exp(math.log(1.0) - 2.9957323 * jax.random.uniform(streams_of[3], (NX, NY, NZ, SLOTS), jnp.float32) ** shard_levels(streams_of[3], (NX, NY, NZ, SLOTS), ((0, 32), (1, 4), (2, 2)), -0.2, 0.2)), 0.05, 1.0),
        "right_side": draw_right_side(jax.random.fold_in(streams_of[7], 71), 0),
        "deflation": bell_draw(streams_of[5], (NDEF, NX, NY, NZ, SLOTS), (0.7 / (CX * CY * CZ * SLOTS * NDEF) ** 0.25), 0.5, ((1, 32), (2, 4), (3, 2)), jnp.float32),
        "coarse_inverse": draw_coarse_inverse(jax.random.fold_in(streams_of[7], 71), 0),
    }


def pair_weights(centre, beside, shifts):
    delta_first = beside[0][..., None, :] + shifts[0] - centre[0][..., :, None]
    delta_second = beside[1][..., None, :] + shifts[1] - centre[1][..., :, None]
    delta_third = beside[2][..., None, :] + shifts[2] - centre[2][..., :, None]
    squared = delta_first * delta_first + delta_second * delta_second + delta_third * delta_third
    radius = jnp.sqrt(squared)
    falloff = jnp.maximum(1.0 - radius, 0.0)
    weight = 20.0 * squared * falloff * falloff * falloff / (squared + 0.01) / SLOTS
    weight = weight * centre[3][..., :, None] * beside[3][..., None, :]
    return weight * (0.5 * (centre[4][..., :, None] + beside[4][..., None, :]))

def plane_sum(padded_geometry, padded_field):
    centre = padded_geometry[:, 1:-1, 1:-1, 1:-1, :]
    extent = centre.shape
    blank_sum = jnp.zeros(extent[1:], jnp.float32)

    def visit(offset_index, running):
        offset_index = jnp.asarray(offset_index).astype(jnp.int32)
        first_shift = (offset_index // 9).astype(jnp.int32)
        second_shift = (offset_index // 3 % 3).astype(jnp.int32)
        third_shift = (offset_index % 3).astype(jnp.int32)
        zero_start = jnp.zeros((), jnp.int32)
        beside = lax.dynamic_slice(padded_geometry, (zero_start, first_shift, second_shift, third_shift, zero_start), extent)
        shifts = ((first_shift - 1).astype(jnp.float32), (second_shift - 1).astype(jnp.float32), (third_shift - 1).astype(jnp.float32))
        weight = pair_weights(centre, beside, shifts)
        if padded_field is None:
            return running + lax.optimization_barrier(jnp.sum(weight, -1))
        beside_field = lax.dynamic_slice(padded_field, (first_shift, second_shift, third_shift, zero_start), extent[1:])
        centre_field = padded_field[1:-1, 1:-1, 1:-1, :]
        return running + lax.optimization_barrier(jnp.sum(weight * (centre_field[..., :, None] - beside_field[..., None, :]), -1))
    return lax.fori_loop(0, 27, visit, blank_sum)

def neighbour_sum(padded_geometry, padded_field):
    plane_count = padded_geometry.shape[1] - 2

    def one_plane(plane_index):
        plane_index = jnp.asarray(plane_index).astype(jnp.int32)
        geometry_slab = lax.dynamic_slice_in_dim(padded_geometry, plane_index, 3, 1)
        if padded_field is None:
            return plane_sum(geometry_slab, None)
        field_slab = lax.dynamic_slice_in_dim(padded_field, plane_index, 3, 0)
        return plane_sum(geometry_slab, field_slab)
    planes = lax.map(one_plane, jnp.arange(plane_count, dtype=jnp.int32))
    return planes[:, 0]

def reference(offsets, counts, correction, dirichlet, right_side, deflation, coarse_inverse):
    slot_index = jnp.arange(SLOTS, dtype=jnp.int32)
    live_mask = (slot_index < counts[..., None]).astype(jnp.float32)
    geometry = jnp.concatenate([offsets, live_mask[None], correction[None]], 0)
    padded_geometry = jnp.pad(geometry, ((0, 0), (1, 1), (1, 1), (1, 1), (0, 0)))
    diagonal = dirichlet + neighbour_sum(padded_geometry, None)
    blocked_basis = deflation.reshape(NDEF, N_GX, CX, N_GY, CY, N_GZ, CZ, SLOTS)

    def apply_matrix(field):
        padded_field = jnp.pad(field, ((1, 1), (1, 1), (1, 1), (0, 0)))
        return live_mask * dirichlet * field + neighbour_sum(padded_geometry, padded_field)

    def precondition(current):
        blocked = current.reshape(N_GX, CX, N_GY, CY, N_GZ, CZ, SLOTS)
        coefficient = jnp.einsum('kaxbyczs,axbyczs->abck', blocked_basis, blocked, precision=lax.Precision.HIGHEST).reshape(COARSE)
        coarse_value = jnp.dot(coarse_inverse, coefficient, precision=lax.Precision.HIGHEST).reshape(N_GX, N_GY, N_GZ, NDEF)
        lifted = jnp.einsum('kaxbyczs,abck->axbyczs', blocked_basis, coarse_value, precision=lax.Precision.HIGHEST).reshape(NX, NY, NZ, SLOTS)
        return live_mask * (current / diagonal + lifted)
    residual = right_side * live_mask
    pressure = jnp.zeros_like(residual)
    smoothed = precondition(residual)
    direction = smoothed
    inner_now = jnp.sum(residual * smoothed)

    def iterate(step_number, state_tuple):
        pressure, residual, direction, inner_now = state_tuple
        product_field = apply_matrix(direction)
        step_size = inner_now / jnp.sum(direction * product_field)
        pressure = pressure + step_size * direction
        residual = residual - step_size * product_field
        smoothed = precondition(residual)
        inner_next = jnp.sum(residual * smoothed)
        direction = smoothed + inner_next / inner_now * direction
        return (pressure, residual, direction, inner_next)
    pressure, residual, direction, inner_now = lax.fori_loop(0, ITERS, iterate, (pressure, residual, direction, inner_now))
    return (pressure, residual, direction)
```

```python
import jax
import jax.numpy as jnp
from jax import lax
from jax.experimental import pallas as pl
from jax.experimental.pallas import tpu as pltpu
from jax.sharding import PartitionSpec as P

SLOTS = 128
FAR = 1000.0

VM = pl.BlockSpec(memory_space=pltpu.VMEM)
SM = pl.BlockSpec(memory_space=pltpu.SMEM)


def f32(*shape):
    return jax.ShapeDtypeStruct(shape, jnp.float32)


def call(kernel, outs, ins, scratch=(), limit=None):
    return pl.pallas_call(
        kernel,
        out_shape=outs,
        in_specs=ins,
        out_specs=jax.tree.map(lambda _: VM, outs),
        scratch_shapes=scratch,
        compiler_params=pltpu.CompilerParams(vmem_limit_bytes=limit),
    )


def project(basis_ref, field, part_ref, second):
    for k in range(64):
        prod = basis_ref[k, 0] * field[0] + basis_ref[k, 1] * field[1]
        part_ref[k : k + 1, :] = jnp.sum(prod, axis=0, keepdims=True)
    row = jnp.sum(part_ref[...].T, axis=0, keepdims=True)
    both = jnp.concatenate([row, row], axis=1)
    lane = lax.broadcasted_iota(jnp.int32, (1, SLOTS), 1)
    return jnp.where((lane >= 64) == (second == 1), both, 0.0)


def inner_row(pairs):
    lane = lax.broadcasted_iota(jnp.int32, (1, SLOTS), 1)
    row = jnp.zeros((1, SLOTS), jnp.float32)
    for at, (left, right) in enumerate(pairs):
        total = jnp.sum(left * right)
        row = jnp.where(lane == at, total, row)
    return row


def prepare_kernel(second_ref, counts_ref, right_ref, basis_ref, live_ref, residual_ref, payload_ref, part_ref):
    slot = lax.broadcasted_iota(jnp.int32, (1, SLOTS), 1)
    for y in range(2):
        for z in range(8):
            live_ref[y, z : z + 1, :] = jnp.where(slot < counts_ref[y * 8 + z], 1.0, 0.0)
    residual_ref[...] = right_ref[...] * live_ref[...]
    payload_ref[...] = project(basis_ref, residual_ref[...], part_ref, second_ref[0])


def assemble(own, before, after, below, above, across, second, put):
    for x, block in enumerate((before, own, after)):
        for y in range(4):
            if y == 0:
                rows = below(x)
            elif y == 3:
                rows = above(x)
            else:
                rows = block(y - 1)
            for z in range(8):
                put(x, y, z + 1, rows[z : z + 1])
            row = across(x * 4 + y)
            put(x, y, 0, jnp.where(second == 1, row, 0.0))
            put(x, y, 9, jnp.where(second == 0, row, 0.0))


def weights_kernel(
    second_ref, counts_ref, own_ref, before_ref, after_ref, below_ref, above_ref, across_ref,
    live_ref, dirichlet_ref, weight_ref, diagonal_ref, inverse_ref, near_ref, mine_ref, sums_ref,
):
    second = second_ref[0]
    tile = (8, SLOTS)
    for f in range(4):
        def put(x, y, z, row, f=f):
            if f == 3:
                near_ref[3, x, y, z] = jnp.broadcast_to(row, tile)
            else:
                near_ref[f, x, y, z] = jnp.broadcast_to(row + float((x, y, z)[f]), tile)

        assemble(
            lambda y: own_ref[f, y], lambda y: before_ref[f, y], lambda y: after_ref[f, y],
            lambda x: below_ref[f, x], lambda x: above_ref[f, x],
            lambda at: across_ref[f, at : at + 1], second, put,
        )
    dead = near_ref[3] == 0.0
    near_ref[0] = jnp.where(dead, FAR, near_ref[0])

    def one_cell(cell, _):
        y, z = cell // 8, cell % 8
        groups = (counts_ref[cell] + 7) // 8
        for f in range(4):
            row = near_ref[f, 1, y + 1, z + 1]
            if f == 0:
                row = jnp.where(near_ref[3, 1, y + 1, z + 1] == 0.0, -FAR, row)
            mine_ref[f] = jnp.broadcast_to(row.T[:, 0:1], (SLOTS, SLOTS))
        sums_ref[...] = jnp.zeros((SLOTS, SLOTS), jnp.float32)

        def one_group(group, _):
            here = pl.ds(pl.multiple_of(group * 8, 8), 8)
            mx, my, mz, mc = (mine_ref[f, here, :] for f in range(4))
            total = jnp.zeros(tile, jnp.float32)
            for at in range(27):
                a, b, c = at // 9, at // 3 % 3, at % 3
                dx = near_ref[0, a, y + b, z + c] - mx
                dy = near_ref[1, a, y + b, z + c] - my
                dz = near_ref[2, a, y + b, z + c] - mz
                square = dx * dx + dy * dy + dz * dz
                radius = square * lax.rsqrt(jnp.maximum(square, 1e-30))
                fall = jnp.maximum(1.0 - radius, 0.0)
                weight = (square * fall) * (fall * fall) / (square + 0.01)
                weight = weight * (near_ref[3, a, y + b, z + c] + mc)
                weight_ref[cell, group, at] = weight
                total = total + weight
            sums_ref[here, :] = total
            return 0

        lax.fori_loop(0, groups, one_group, 0)
        sums = jnp.sum(sums_ref[...].T, axis=0, keepdims=True)
        diagonal_ref[y, pl.ds(z, 1), :] = sums
        return 0

    lax.fori_loop(0, 16, one_cell, 0)
    sums = diagonal_ref[...]
    inverse_ref[...] = live_ref[...] / (dirichlet_ref[...] + sums)
    diagonal_ref[...] = live_ref[...] * dirichlet_ref[...] + sums


def coarse_lift(values_ref, coarse_ref, basis_ref, part_ref):
    total = jnp.zeros((64, SLOTS), jnp.float32)
    for t in range(128):
        total = total + coarse_ref[:, t * SLOTS : (t + 1) * SLOTS] * values_ref[t : t + 1, :]
    part_ref[...] = jnp.broadcast_to(jnp.sum(total, axis=1, keepdims=True), (64, SLOTS))
    sums = [[jnp.zeros((8, SLOTS), jnp.float32) for _ in range(2)] for _ in range(2)]
    for k in range(64):
        scale = jnp.broadcast_to(part_ref[k : k + 1, :], (8, SLOTS))
        for y in range(2):
            sums[k % 2][y] = sums[k % 2][y] + scale * basis_ref[k, y]
    return jnp.stack([sums[0][y] + sums[1][y] for y in range(2)])


def total_of(gathered_ref, at):
    rows = gathered_ref[pl.ds(1, 128, stride=2), :]
    lane = lax.broadcasted_iota(jnp.int32, rows.shape, 1)
    return jnp.sum(jnp.where(lane == at, rows, 0.0))


def first_smooth_kernel(gathered_ref, coarse_ref, basis_ref, live_ref, residual_ref, inverse_ref, smoothed_ref, part_ref):
    lifted = coarse_lift(gathered_ref, coarse_ref, basis_ref, part_ref)
    smoothed_ref[...] = residual_ref[...] * inverse_ref[...] + live_ref[...] * lifted


def second_smooth_kernel(
    gathered_ref, coefficient_ref, coarse_ref, basis_ref, live_ref, residual_ref, inverse_ref,
    smoothed_ref, image_ref, new_coefficient_ref, new_residual_ref, new_smoothed_ref, part_ref,
):
    step = total_of(gathered_ref, 0) / total_of(gathered_ref, 1)
    new_coefficient_ref[...] = coefficient_ref[...] - step * gathered_ref[pl.ds(0, 128, stride=2), :]
    lifted = coarse_lift(new_coefficient_ref, coarse_ref, basis_ref, part_ref)
    residual = residual_ref[...] - step * image_ref[...]
    new_residual_ref[...] = residual
    new_smoothed_ref[...] = residual * inverse_ref[...] + live_ref[...] * lifted


def third_smooth_kernel(
    gathered_ref, before_ref, coefficient_ref, coarse_ref, basis_ref, live_ref, residual_ref, inverse_ref,
    first_ref, first_image_ref, smoothed_ref, image_ref,
    pressure_ref, new_residual_ref, new_smoothed_ref, direction_ref, payload_ref, values_ref, part_ref,
):
    inner_first, curve_first = total_of(before_ref, 0), total_of(before_ref, 1)
    inner, curve = total_of(gathered_ref, 0), total_of(gathered_ref, 1)
    cross = total_of(gathered_ref, 2) + total_of(gathered_ref, 3)
    step_first = inner_first / curve_first
    ratio = inner / inner_first
    step = inner / (curve + ratio * (cross + ratio * curve_first))
    values_ref[...] = coefficient_ref[...] - step * (
        gathered_ref[pl.ds(0, 128, stride=2), :] + ratio * before_ref[pl.ds(0, 128, stride=2), :]
    )
    lifted = coarse_lift(values_ref, coarse_ref, basis_ref, part_ref)
    direction = smoothed_ref[...] + ratio * first_ref[...]
    direction_ref[...] = direction
    pressure_ref[...] = step_first * first_ref[...] + step * direction
    residual = residual_ref[...] - step * (image_ref[...] + ratio * first_image_ref[...])
    new_residual_ref[...] = residual
    smoothed = residual * inverse_ref[...] + live_ref[...] * lifted
    new_smoothed_ref[...] = smoothed
    payload_ref[...] = inner_row([(residual, smoothed), (residual_ref[...], smoothed_ref[...])])


def image_kernel(
    second_ref, counts_ref, weight_ref, own_ref, before_ref, after_ref, below_ref, above_ref, across_ref,
    diagonal_ref, residual_ref, basis_ref, *rest,
):
    olds, (image_ref, payload_ref, near_ref, sums_ref, part_ref) = rest[:-5], rest[-5:]
    second = second_ref[0]
    tile = (8, SLOTS)

    def put(x, y, z, row):
        near_ref[x, y, z] = jnp.broadcast_to(row, tile)

    assemble(
        lambda y: own_ref[y], lambda y: before_ref[y], lambda y: after_ref[y],
        lambda x: below_ref[x], lambda x: above_ref[x],
        lambda at: across_ref[at : at + 1], second, put,
    )

    def one_cell(cell, _):
        y, z = cell // 8, cell % 8
        groups = (counts_ref[cell] + 7) // 8
        sums_ref[...] = jnp.zeros((SLOTS, SLOTS), jnp.float32)

        def one_group(group, _):
            parts = [jnp.zeros(tile, jnp.float32) for _ in range(3)]
            for at in range(27):
                a, b, c = at // 9, at // 3 % 3, at % 3
                parts[at % 3] = parts[at % 3] + weight_ref[cell, group, at] * near_ref[a, y + b, z + c]
            sums_ref[pl.ds(pl.multiple_of(group * 8, 8), 8), :] = parts[0] + parts[1] + parts[2]
            return 0

        lax.fori_loop(0, groups, one_group, 0)
        image_ref[y, pl.ds(z, 1), :] = jnp.sum(sums_ref[...].T, axis=0, keepdims=True)
        return 0

    lax.fori_loop(0, 16, one_cell, 0)
    own = own_ref[...]
    image = diagonal_ref[...] * own - image_ref[...]
    image_ref[...] = image
    payload_ref[0:1, :] = project(basis_ref, image, part_ref, second)
    pairs = [(residual_ref[...], own), (own, image)]
    if olds:
        first_ref, first_image_ref = olds
        pairs += [(own, first_image_ref[...]), (first_ref[...], image)]
    payload_ref[1:2, :] = inner_row(pairs)


def steps(axis):
    size = lax.axis_size(axis)
    up = [(i, i + 1) for i in range(size - 1)]
    return up, [(j, i) for i, j in up]


def around(field, second):
    up, down = steps("gx")
    before = lax.ppermute(field, "gx", up)
    after = lax.ppermute(field, "gx", down)
    three = jnp.stack([before, field, after], axis=-4)
    up, down = steps("gy")
    below = lax.ppermute(three[..., :, 1, :, :], "gy", up)
    above = lax.ppermute(three[..., :, 0, :, :], "gy", down)
    full = jnp.concatenate([below[..., :, None, :, :], three, above[..., :, None, :, :]], axis=-3)
    face = jnp.where(second == 0, full[..., 7, :], full[..., 0, :])
    face = face.reshape(face.shape[:-3] + (12, SLOTS))
    across = lax.ppermute(face, "gz", [(0, 1), (1, 0)])
    return before, after, below, above, across


def gather(payload):
    both = payload + lax.ppermute(payload, "gz", [(0, 1), (1, 0)])
    rows = payload.shape[0]
    spread = jnp.broadcast_to(both[None], (128, rows, SLOTS))
    got = lax.all_to_all(spread, ("gx", "gy"), 0, 0, tiled=True)
    return got.reshape(128 * rows, SLOTS)


def per_device(offsets, counts, correction, dirichlet, right_side, deflation, coarse_inverse):
    second = lax.axis_index("gz").astype(jnp.int32)
    second_ref = second.reshape(1)
    cell_counts = counts.reshape(16)
    block = lambda x: x.reshape(2, 8, SLOTS)
    offsets = offsets.reshape(3, 2, 8, SLOTS)
    dirichlet, right_side = block(dirichlet), block(right_side)
    basis = deflation.reshape(64, 2, 8, SLOTS)
    cells = f32(2, 8, SLOTS)

    live, residual, payload = call(
        prepare_kernel, (cells, cells, f32(1, SLOTS)), [SM, SM, VM, VM], [pltpu.VMEM((64, SLOTS), jnp.float32)]
    )(second_ref, cell_counts, right_side, basis)
    scaled = (block(correction) * live) * (10.0 / SLOTS)
    geometry = jnp.concatenate([offsets, scaled[None]], 0)
    halo = around(geometry, second)
    coefficient = gather(payload)
    part = pltpu.VMEM((64, SLOTS), jnp.float32)

    weight, diagonal, inverse = call(
        weights_kernel,
        (f32(16, 16, 27, 8, SLOTS), cells, cells),
        [SM, SM] + [VM] * 8,
        [
            pltpu.VMEM((4, 3, 4, 10, 8, SLOTS), jnp.float32),
            pltpu.VMEM((4, SLOTS, SLOTS), jnp.float32),
            pltpu.VMEM((SLOTS, SLOTS), jnp.float32),
        ],
        limit=56 * 2**20,
    )(second_ref, cell_counts, geometry, *halo, live, dirichlet)

    def image_of(field, residual, *olds):
        return call(
            image_kernel,
            (cells, f32(2, SLOTS)),
            [SM, SM] + [VM] * (10 + len(olds)),
            [
                pltpu.VMEM((3, 4, 10, 8, SLOTS), jnp.float32),
                pltpu.VMEM((SLOTS, SLOTS), jnp.float32),
                part,
            ],
            limit=56 * 2**20,
        )(second_ref, cell_counts, weight, field, *around(field, second), diagonal, residual, basis, *olds)

    smoothed = call(first_smooth_kernel, cells, [VM] * 6, [part])(
        coefficient, coarse_inverse, basis, live, residual, inverse
    )
    image, payload = image_of(smoothed, residual)
    gathered_first = gather(payload)
    coefficient, residual, second_smoothed = call(
        second_smooth_kernel, (f32(128, SLOTS), cells, cells), [VM] * 9, [part]
    )(gathered_first, coefficient, coarse_inverse, basis, live, residual, inverse, smoothed, image)
    second_image, payload = image_of(second_smoothed, residual, smoothed, image)
    gathered = gather(payload)
    pressure, residual, third_smoothed, direction, payload = call(
        third_smooth_kernel,
        (cells, cells, cells, cells, f32(1, SLOTS)),
        [VM] * 12,
        [pltpu.VMEM((128, SLOTS), jnp.float32), part],
    )(
        gathered, gathered_first, coefficient, coarse_inverse, basis, live, residual, inverse,
        smoothed, image, second_smoothed, second_image,
    )
    totals = jnp.sum(gather(payload), axis=0)
    direction = third_smoothed + totals[0] / totals[1] * direction
    shape = (1, 2, 8, SLOTS)
    return pressure.reshape(shape), residual.reshape(shape), direction.reshape(shape)


def solution(mesh):
    field = P("gx", "gy", "gz", None)
    in_specs = (
        P(None, "gx", "gy", "gz", None),
        P("gx", "gy", "gz"),
        field,
        field,
        field,
        P(None, "gx", "gy", "gz", None),
        P(("gx", "gy", "gz"), None),
    )
    return jax.shard_map(per_device, mesh=mesh, in_specs=in_specs, out_specs=(field,) * 3, check_vma=False)
```

```python
import jax
import jax.numpy as jnp
from jax import lax
from jax.experimental import pallas as pl
from jax.experimental.pallas import tpu as pltpu
from jax.sharding import PartitionSpec as P

SLOTS = 128
FAR = 1000.0
LIMIT = 4 * 2**20

VM = pl.BlockSpec(memory_space=pltpu.VMEM)
SM = pl.BlockSpec(memory_space=pltpu.SMEM)
ANY = pl.BlockSpec(memory_space=pl.ANY)


def f32(*shape):
    return jax.ShapeDtypeStruct(shape, jnp.float32)


def call(kernel, outs, ins, scratch=(), limit=LIMIT):
    return pl.pallas_call(
        kernel,
        out_shape=outs,
        in_specs=ins,
        out_specs=jax.tree.map(lambda _: VM, outs),
        scratch_shapes=scratch,
        compiler_params=pltpu.CompilerParams(vmem_limit_bytes=limit),
    )


def project(basis_ref, field, part_ref, second):
    for k in range(64):
        prod = basis_ref[k, 0] * field[0] + basis_ref[k, 1] * field[1]
        part_ref[k : k + 1, :] = jnp.sum(prod, axis=0, keepdims=True)
    row = jnp.sum(part_ref[...].T, axis=0, keepdims=True)
    both = jnp.concatenate([row, row], axis=1)
    lane = lax.broadcasted_iota(jnp.int32, (1, SLOTS), 1)
    return jnp.where((lane >= 64) == (second == 1), both, 0.0)


def inner_row(pairs):
    lane = lax.broadcasted_iota(jnp.int32, (1, SLOTS), 1)
    row = jnp.zeros((1, SLOTS), jnp.float32)
    for at, (left, right) in enumerate(pairs):
        total = jnp.sum(left * right)
        row = jnp.where(lane == at, total, row)
    return row


def fetch(pairs, sems):
    copies = [pltpu.make_async_copy(src, dst, sems.at[at]) for at, (src, dst) in enumerate(pairs)]
    for copy in copies:
        copy.start()
    return copies


def prepare_kernel(
    second_ref, counts_hbm, offsets_hbm, correction_hbm, right_hbm, dirichlet_hbm, basis_hbm,
    geometry_ref, live_ref, residual_ref, payload_ref, counts_ref, dirichlet_ref, basis_ref,
    counts_smem, offsets_ref, correction_ref, right_ref, part_ref, sems,
):
    copies = fetch(
        (
            (counts_hbm, counts_smem), (counts_hbm, counts_ref), (offsets_hbm, offsets_ref),
            (correction_hbm, correction_ref), (right_hbm, right_ref), (dirichlet_hbm, dirichlet_ref),
            (basis_hbm, basis_ref),
        ),
        sems,
    )
    for copy in copies[:-1]:
        copy.wait()
    slot = lax.broadcasted_iota(jnp.int32, (1, SLOTS), 1)
    for y in range(2):
        for z in range(8):
            live_ref[y, z : z + 1, :] = jnp.where(slot < counts_smem[0, y, z], 1.0, 0.0)
    live = live_ref[...]
    geometry_ref[0:3] = offsets_ref[...]
    geometry_ref[3] = correction_ref[...] * live * (10.0 / SLOTS)
    residual_ref[...] = right_ref[...] * live
    copies[-1].wait()
    payload_ref[...] = project(basis_ref, residual_ref[...], part_ref, second_ref[0])


def side_faces_kernel(before_ref, field_ref, after_ref, up_ref, down_ref):
    for f in range(field_ref.shape[0]):
        for x, ref in enumerate((before_ref, field_ref, after_ref)):
            up_ref[f, x] = ref[f, 1]
            down_ref[f, x] = ref[f, 0]


def top_face_kernel(second_ref, before_ref, field_ref, after_ref, below_ref, above_ref, face_ref):
    second = second_ref[0]

    def pick(rows):
        return jnp.where(second == 0, rows[7:8], rows[0:1])

    for f in range(field_ref.shape[0]):
        for x, ref in enumerate((before_ref, field_ref, after_ref)):
            for y, rows in enumerate((below_ref[f, x], ref[f, 0], ref[f, 1], above_ref[f, x])):
                face_ref[f, x * 4 + y : x * 4 + y + 1, :] = pick(rows)


def spread_kernel(mine_ref, theirs_ref, spread_ref):
    rows = mine_ref[...] + theirs_ref[...]
    spread_ref[...] = jnp.broadcast_to(rows[None], spread_ref.shape)


def finish_kernel(gathered_ref, smoothed_ref, direction_ref, out_ref):
    rows = gathered_ref[...]
    lane = lax.broadcasted_iota(jnp.int32, rows.shape, 1)
    inner = jnp.sum(jnp.where(lane == 0, rows, 0.0))
    before = jnp.sum(jnp.where(lane == 1, rows, 0.0))
    out_ref[...] = smoothed_ref[...] + inner / before * direction_ref[...]


def assemble(own, before, after, below, above, across, second, put):
    for x, block in enumerate((before, own, after)):
        for y in range(4):
            if y == 0:
                rows = below(x)
            elif y == 3:
                rows = above(x)
            else:
                rows = block(y - 1)
            for z in range(8):
                put(x, y, z + 1, rows[z : z + 1])
            row = across(x * 4 + y)
            put(x, y, 0, jnp.where(second == 1, row, 0.0))
            put(x, y, 9, jnp.where(second == 0, row, 0.0))


def row_sums(sums_ref, out_ref):
    for cell in range(16):
        out_ref[cell // 8, cell % 8 : cell % 8 + 1, :] = jnp.sum(sums_ref[cell].T, axis=0, keepdims=True)


def weights_kernel(
    second_ref, counts_ref, own_ref, before_ref, after_ref, below_ref, above_ref, across_ref,
    live_ref, dirichlet_ref, coarse_hbm,
    weight_a, weight_b, weight_c, diagonal_ref, inverse_ref, coarse_ref, near_ref, mine_ref, sums_ref, sems,
):
    copies = fetch(((coarse_hbm, coarse_ref),), sems)
    weight_refs = (weight_a, weight_b, weight_c)
    second = second_ref[0]
    tile = (8, SLOTS)
    for f in range(4):
        def put(x, y, z, row, f=f):
            if f == 3:
                near_ref[3, x, y, z] = jnp.broadcast_to(row, tile)
            else:
                near_ref[f, x, y, z] = jnp.broadcast_to(row + float((x, y, z)[f]), tile)

        assemble(
            lambda y: own_ref[f, y], lambda y: before_ref[f, y], lambda y: after_ref[f, y],
            lambda x: below_ref[f, x], lambda x: above_ref[f, x],
            lambda at: across_ref[f, at : at + 1], second, put,
        )
    dead = near_ref[3] == 0.0
    near_ref[0] = jnp.where(dead, FAR, near_ref[0])

    cell_row = lax.broadcasted_iota(jnp.int32, (16, SLOTS), 0)
    scale = own_ref[3].reshape(16, SLOTS)
    fields = (
        jnp.where(scale == 0.0, -FAR, own_ref[0].reshape(16, SLOTS) + 1.0),
        own_ref[1].reshape(16, SLOTS) + jnp.where(cell_row >= 8, 2.0, 1.0),
        own_ref[2].reshape(16, SLOTS) + (jnp.where(cell_row >= 8, cell_row - 8, cell_row) + 1).astype(jnp.float32),
        scale,
    )
    for f, field in enumerate(fields):
        columns = field.T
        for cell in range(16):
            mine_ref[cell, f] = jnp.broadcast_to(columns[:, cell : cell + 1], (SLOTS, SLOTS))

    def one_cell(y, z):
        cell = y * 8 + z
        groups = (counts_ref[0, y, z] + 7) >> 3

        def some_groups(first, count):
            spots = [pl.ds(pl.multiple_of((first + g) * 8, 8), 8) for g in range(count)]
            mine = [[mine_ref[cell, f, spot, :] for f in range(4)] for spot in spots]
            totals = [jnp.zeros(tile, jnp.float32) for _ in spots]
            for at in range(27):
                a, b, c = at // 9, at // 3 % 3, at % 3
                near = [near_ref[f, a, y + b, z + c] for f in range(4)]
                for g in range(count):
                    dx, dy, dz = (near[f] - mine[g][f] for f in range(3))
                    square = dx * dx + dy * dy + dz * dz
                    radius = square * lax.rsqrt(jnp.maximum(square, 1e-30))
                    fall = jnp.maximum(1.0 - radius, 0.0)
                    weight = (square * fall) * (fall * fall) / (square + 0.01)
                    weight = weight * (near[3] + mine[g][3])
                    weight_refs[a][cell, first + g, at % 9] = weight
                    totals[g] = totals[g] + weight
            for g in range(count):
                sums_ref[cell, spots[g], :] = totals[g]

        def two_groups(pair, _):
            some_groups(pair * 2, 2)
            return 0

        lax.fori_loop(0, groups >> 1, two_groups, 0)

        @pl.when((groups & 1) == 1)
        def _():
            some_groups(groups - 1, 1)

    for y in range(2):
        def cell_of(z, _, y=y):
            one_cell(y, z)
            return 0

        lax.fori_loop(0, 8, cell_of, 0)

    row_sums(sums_ref, diagonal_ref)
    live = live_ref[...]
    sums = jnp.where(live == 0.0, 0.0, diagonal_ref[...])
    inverse_ref[...] = live / (dirichlet_ref[...] + sums)
    diagonal_ref[...] = live * dirichlet_ref[...] + sums
    copies[0].wait()


def coarse_lift(values_ref, coarse_ref, basis_ref, part_ref):
    total = jnp.zeros((64, SLOTS), jnp.float32)
    for t in range(128):
        total = total + coarse_ref[:, t * SLOTS : (t + 1) * SLOTS] * values_ref[t : t + 1, :]
    part_ref[...] = jnp.broadcast_to(jnp.sum(total, axis=1, keepdims=True), (64, SLOTS))
    sums = [[jnp.zeros((8, SLOTS), jnp.float32) for _ in range(2)] for _ in range(2)]
    for k in range(64):
        scale = jnp.broadcast_to(part_ref[k : k + 1, :], (8, SLOTS))
        for y in range(2):
            sums[k % 2][y] = sums[k % 2][y] + scale * basis_ref[k, y]
    return jnp.stack([sums[0][y] + sums[1][y] for y in range(2)])


def total_of(gathered_ref, at):
    rows = gathered_ref[pl.ds(1, 128, stride=2), :]
    lane = lax.broadcasted_iota(jnp.int32, rows.shape, 1)
    return jnp.sum(jnp.where(lane == at, rows, 0.0))


def first_smooth_kernel(gathered_ref, coarse_ref, basis_ref, live_ref, residual_ref, inverse_ref, smoothed_ref, part_ref):
    lifted = coarse_lift(gathered_ref, coarse_ref, basis_ref, part_ref)
    smoothed_ref[...] = residual_ref[...] * inverse_ref[...] + live_ref[...] * lifted


def second_smooth_kernel(
    gathered_ref, coefficient_ref, coarse_ref, basis_ref, live_ref, residual_ref, inverse_ref,
    smoothed_ref, image_ref, new_coefficient_ref, new_residual_ref, new_smoothed_ref, part_ref,
):
    step = total_of(gathered_ref, 0) / total_of(gathered_ref, 1)
    new_coefficient_ref[...] = coefficient_ref[...] - step * gathered_ref[pl.ds(0, 128, stride=2), :]
    lifted = coarse_lift(new_coefficient_ref, coarse_ref, basis_ref, part_ref)
    residual = residual_ref[...] - step * image_ref[...]
    new_residual_ref[...] = residual
    new_smoothed_ref[...] = residual * inverse_ref[...] + live_ref[...] * lifted


def third_smooth_kernel(
    gathered_ref, before_ref, coefficient_ref, coarse_ref, basis_ref, live_ref, residual_ref, inverse_ref,
    first_ref, first_image_ref, smoothed_ref, image_ref,
    pressure_ref, new_residual_ref, new_smoothed_ref, direction_ref, payload_ref, values_ref, part_ref,
):
    inner_first, curve_first = total_of(before_ref, 0), total_of(before_ref, 1)
    inner, curve = total_of(gathered_ref, 0), total_of(gathered_ref, 1)
    cross = total_of(gathered_ref, 2) + total_of(gathered_ref, 3)
    step_first = inner_first / curve_first
    ratio = inner / inner_first
    step = inner / (curve + ratio * (cross + ratio * curve_first))
    values_ref[...] = coefficient_ref[...] - step * (
        gathered_ref[pl.ds(0, 128, stride=2), :] + ratio * before_ref[pl.ds(0, 128, stride=2), :]
    )
    lifted = coarse_lift(values_ref, coarse_ref, basis_ref, part_ref)
    direction = smoothed_ref[...] + ratio * first_ref[...]
    direction_ref[...] = direction
    pressure_ref[...] = step_first * first_ref[...] + step * direction
    residual = residual_ref[...] - step * (image_ref[...] + ratio * first_image_ref[...])
    new_residual_ref[...] = residual
    smoothed = residual * inverse_ref[...] + live_ref[...] * lifted
    new_smoothed_ref[...] = smoothed
    payload_ref[...] = inner_row([(residual, smoothed), (residual_ref[...], smoothed_ref[...])])


def image_kernel(
    second_ref, counts_ref, weight_a, weight_b, weight_c, own_ref, before_ref, after_ref, below_ref, above_ref,
    across_ref, live_ref, diagonal_ref, residual_ref, basis_ref, *rest,
):
    weight_refs = (weight_a, weight_b, weight_c)
    olds, (image_ref, payload_ref, near_ref, sums_ref, part_ref) = rest[:-5], rest[-5:]
    second = second_ref[0]
    tile = (8, SLOTS)

    def put(x, y, z, row):
        near_ref[x, y, z] = jnp.broadcast_to(row, tile)

    assemble(
        lambda y: own_ref[y], lambda y: before_ref[y], lambda y: after_ref[y],
        lambda x: below_ref[x], lambda x: above_ref[x],
        lambda at: across_ref[at : at + 1], second, put,
    )

    def one_cell(y, z):
        cell = y * 8 + z

        def two_groups(pair, _):
            parts = [[jnp.zeros(tile, jnp.float32) for _ in range(3)] for _ in range(2)]
            for at in range(27):
                a, b, c = at // 9, at // 3 % 3, at % 3
                near = near_ref[a, y + b, z + c]
                for g in range(2):
                    parts[g][at % 3] = parts[g][at % 3] + weight_refs[a][cell, pair * 2 + g, at % 9] * near
            for g in range(2):
                spot = pl.ds(pl.multiple_of((pair * 2 + g) * 8, 8), 8)
                sums_ref[cell, spot, :] = parts[g][0] + parts[g][1] + parts[g][2]
            return 0

        lax.fori_loop(0, (counts_ref[0, y, z] + 15) >> 4, two_groups, 0)

    for y in range(2):
        def cell_of(z, _, y=y):
            one_cell(y, z)
            return 0

        lax.fori_loop(0, 8, cell_of, 0)

    row_sums(sums_ref, image_ref)
    own = own_ref[...]
    image = jnp.where(live_ref[...] == 0.0, 0.0, diagonal_ref[...] * own - image_ref[...])
    image_ref[...] = image
    payload_ref[0:1, :] = project(basis_ref, image, part_ref, second)
    pairs = [(residual_ref[...], own), (own, image)]
    if olds:
        first_ref, first_image_ref = olds
        pairs += [(own, first_image_ref[...]), (first_ref[...], image)]
    payload_ref[1:2, :] = inner_row(pairs)


def steps(axis):
    size = lax.axis_size(axis)
    up = [(i, i + 1) for i in range(size - 1)]
    return up, [(j, i) for i, j in up]


def around(field, second):
    count = field.shape[0]
    up, down = steps("gx")
    before = lax.ppermute(field, "gx", up)
    after = lax.ppermute(field, "gx", down)
    side = f32(count, 3, 8, SLOTS)
    upper, lower = call(side_faces_kernel, (side, side), [VM] * 3)(before, field, after)
    up, down = steps("gy")
    below = lax.ppermute(upper, "gy", up)
    above = lax.ppermute(lower, "gy", down)
    face = call(top_face_kernel, f32(count, 12, SLOTS), [SM] + [VM] * 5)(second, before, field, after, below, above)
    across = lax.ppermute(face, "gz", [(0, 1), (1, 0)])
    return before, after, below, above, across


def gather(payload):
    theirs = lax.ppermute(payload, "gz", [(0, 1), (1, 0)])
    rows = payload.shape[0]
    spread = call(spread_kernel, f32(128, rows, SLOTS), [VM] * 2)(payload, theirs)
    got = lax.all_to_all(spread, ("gx", "gy"), 0, 0, tiled=True)
    return got.reshape(128 * rows, SLOTS)


def per_device(offsets, counts, correction, dirichlet, right_side, deflation, coarse_inverse):
    second = lax.axis_index("gz").astype(jnp.int32)
    second = second.reshape(1)
    block = lambda x: x.reshape(2, 8, SLOTS)
    offsets = offsets.reshape(3, 2, 8, SLOTS)
    dirichlet, right_side, correction = block(dirichlet), block(right_side), block(correction)
    basis = deflation.reshape(64, 2, 8, SLOTS)
    cells = f32(2, 8, SLOTS)

    onchip = lambda x: pltpu.with_memory_space_constraint(x, pltpu.VMEM)
    outside = lambda x: pltpu.with_memory_space_constraint(x, pltpu.HBM)
    vmem = lambda *shape: pltpu.VMEM(shape, jnp.float32)
    part = vmem(64, SLOTS)

    geometry, live, residual, payload, counts, dirichlet, basis = call(
        prepare_kernel,
        (
            f32(4, 2, 8, SLOTS), cells, cells, f32(1, SLOTS),
            pltpu.VMEM((1, 2, 8), jnp.int32), vmem(2, 8, SLOTS), vmem(64, 2, 8, SLOTS),
        ),
        [SM] + [ANY] * 6,
        [
            pltpu.SMEM((1, 2, 8), jnp.int32), vmem(3, 2, 8, SLOTS), vmem(2, 8, SLOTS), vmem(2, 8, SLOTS), part,
            pltpu.SemaphoreType.DMA((7,)),
        ],
    )(second, *map(outside, (counts, offsets, correction, right_side, dirichlet, basis)))
    counts, dirichlet, basis = onchip(counts), onchip(dirichlet), onchip(basis)
    halo = around(geometry, second)
    coefficient = gather(payload)
    coefficient, geometry = lax.optimization_barrier((coefficient, geometry))

    *weights, diagonal, inverse, coarse = call(
        weights_kernel,
        (*(vmem(16, 16, 9, 8, SLOTS),) * 3, cells, cells, vmem(64, 128 * SLOTS)),
        [SM, SM] + [VM] * 8 + [ANY],
        [
            vmem(4, 3, 4, 10, 8, SLOTS), vmem(16, 4, SLOTS, SLOTS), vmem(16, SLOTS, SLOTS),
            pltpu.SemaphoreType.DMA((1,)),
        ],
        limit=8 * 2**20,
    )(second, counts, geometry, *halo, live, dirichlet, outside(coarse_inverse))
    weights, coarse = [onchip(x) for x in weights], onchip(coarse)

    def image_of(field, residual, *olds):
        return call(
            image_kernel,
            (cells, f32(2, SLOTS)),
            [SM, SM] + [VM] * (13 + len(olds)),
            [vmem(3, 4, 10, 8, SLOTS), vmem(16, SLOTS, SLOTS), part],
        )(
            second, counts, *weights, field, *(piece[0] for piece in around(field[None], second)),
            live, diagonal, residual, basis, *olds,
        )

    smoothed = call(first_smooth_kernel, cells, [VM] * 6, [part])(
        coefficient, coarse, basis, live, residual, inverse
    )
    image, payload = image_of(smoothed, residual)
    gathered_first = gather(payload)
    coefficient, residual, second_smoothed = call(
        second_smooth_kernel, (f32(128, SLOTS), cells, cells), [VM] * 9, [part]
    )(gathered_first, coefficient, coarse, basis, live, residual, inverse, smoothed, image)
    second_image, payload = image_of(second_smoothed, residual, smoothed, image)
    gathered = gather(payload)
    pressure, residual, third_smoothed, direction, payload = call(
        third_smooth_kernel,
        (cells, cells, cells, cells, f32(1, SLOTS)),
        [VM] * 12,
        [pltpu.VMEM((128, SLOTS), jnp.float32), part],
    )(
        gathered, gathered_first, coefficient, coarse, basis, live, residual, inverse,
        smoothed, image, second_smoothed, second_image,
    )
    direction = call(finish_kernel, cells, [VM] * 3)(gather(payload), third_smoothed, direction)
    shape = (1, 2, 8, SLOTS)
    return pressure.reshape(shape), residual.reshape(shape), direction.reshape(shape)


def solution(mesh):
    field = P("gx", "gy", "gz", None)
    in_specs = (
        P(None, "gx", "gy", "gz", None),
        P("gx", "gy", "gz"),
        field,
        field,
        field,
        P(None, "gx", "gy", "gz", None),
        P(("gx", "gy", "gz"), None),
    )
    return jax.shard_map(per_device, mesh=mesh, in_specs=in_specs, out_specs=(field,) * 3, check_vma=False)
```

```python
import jax
import jax.numpy as jnp
from jax import lax
from jax.experimental import pallas as pl
from jax.experimental.pallas import tpu as pltpu
from jax.sharding import PartitionSpec as P

SLOTS = 128
FAR = 1000.0
LIMIT = 4 * 2**20

VM = pl.BlockSpec(memory_space=pltpu.VMEM)
SM = pl.BlockSpec(memory_space=pltpu.SMEM)
ANY = pl.BlockSpec(memory_space=pl.ANY)


def f32(*shape):
    return jax.ShapeDtypeStruct(shape, jnp.float32)


def call(kernel, outs, ins, scratch=(), limit=LIMIT):
    return pl.pallas_call(
        kernel,
        out_shape=outs,
        in_specs=ins,
        out_specs=jax.tree.map(lambda _: VM, outs),
        scratch_shapes=scratch,
        compiler_params=pltpu.CompilerParams(vmem_limit_bytes=limit),
    )


def project(basis_ref, field, part_ref, second):
    for k in range(64):
        prod = basis_ref[k, 0] * field[0] + basis_ref[k, 1] * field[1]
        part_ref[k : k + 1, :] = jnp.sum(prod, axis=0, keepdims=True)
    row = jnp.sum(part_ref[...].T, axis=0, keepdims=True)
    both = jnp.concatenate([row, row], axis=1)
    lane = lax.broadcasted_iota(jnp.int32, (1, SLOTS), 1)
    return jnp.where((lane >= 64) == (second == 1), both, 0.0)


def inner_row(pairs):
    lane = lax.broadcasted_iota(jnp.int32, (1, SLOTS), 1)
    row = jnp.zeros((1, SLOTS), jnp.float32)
    for at, (left, right) in enumerate(pairs):
        total = jnp.sum(left * right)
        row = jnp.where(lane == at, total, row)
    return row


def fetch(pairs, sems):
    copies = [pltpu.make_async_copy(src, dst, sems.at[at]) for at, (src, dst) in enumerate(pairs)]
    for copy in copies:
        copy.start()
    return copies


def prepare_kernel(
    second_ref, counts_hbm, offsets_hbm, correction_hbm, right_hbm, dirichlet_hbm, basis_hbm,
    geometry_ref, live_ref, residual_ref, payload_ref, counts_ref, dirichlet_ref, basis_ref,
    counts_smem, offsets_ref, correction_ref, right_ref, part_ref, sems,
):
    copies = fetch(
        (
            (counts_hbm, counts_smem), (counts_hbm, counts_ref), (offsets_hbm, offsets_ref),
            (correction_hbm, correction_ref), (right_hbm, right_ref), (dirichlet_hbm, dirichlet_ref),
            (basis_hbm, basis_ref),
        ),
        sems,
    )
    for copy in copies[:-1]:
        copy.wait()
    slot = lax.broadcasted_iota(jnp.int32, (1, SLOTS), 1)
    for y in range(2):
        for z in range(8):
            live_ref[y, z : z + 1, :] = jnp.where(slot < counts_smem[0, y, z], 1.0, 0.0)
    live = live_ref[...]
    geometry_ref[0:3] = offsets_ref[...]
    geometry_ref[3] = correction_ref[...] * live * (10.0 / SLOTS)
    residual_ref[...] = right_ref[...] * live
    copies[-1].wait()
    payload_ref[...] = project(basis_ref, residual_ref[...], part_ref, second_ref[0])


def top_face_kernel(second_ref, field_ref, face_ref):
    second = second_ref[0]
    for f in range(field_ref.shape[0]):
        for y in range(2):
            rows = field_ref[f, y]
            face_ref[f, y : y + 1, :] = jnp.where(second == 0, rows[7:8], rows[0:1])


def side_faces_kernel(field_ref, across_ref, up_ref, down_ref):
    for f in range(field_ref.shape[0]):
        for y, ref in enumerate((down_ref, up_ref)):
            ref[f, 0] = field_ref[f, y]
            ref[f, 1] = jnp.broadcast_to(across_ref[f, y : y + 1, :], (8, SLOTS))


def block_kernel(field_ref, across_ref, below_ref, above_ref, block_ref):
    for f in range(field_ref.shape[0]):
        block_ref[f, 0] = below_ref[f, 0]
        block_ref[f, 1] = field_ref[f, 0]
        block_ref[f, 2] = field_ref[f, 1]
        block_ref[f, 3] = above_ref[f, 0]
        rows = (below_ref[f, 1, 0:1], across_ref[f, 0:1], across_ref[f, 1:2], above_ref[f, 1, 0:1])
        for y, row in enumerate(rows):
            block_ref[f, 4, y : y + 1, :] = row


def spread_kernel(mine_ref, theirs_ref, spread_ref):
    rows = mine_ref[...] + theirs_ref[...]
    spread_ref[...] = jnp.broadcast_to(rows[None], spread_ref.shape)


def finish_kernel(gathered_ref, smoothed_ref, direction_ref, out_ref):
    rows = gathered_ref[...]
    lane = lax.broadcasted_iota(jnp.int32, rows.shape, 1)
    inner = jnp.sum(jnp.where(lane == 0, rows, 0.0))
    before = jnp.sum(jnp.where(lane == 1, rows, 0.0))
    out_ref[...] = smoothed_ref[...] + inner / before * direction_ref[...]


def assemble(block, second, put):
    for y in range(4):
        rows = block(y)
        for z in range(8):
            put(y, z + 1, rows[z : z + 1])
        row = block(4)[y : y + 1]
        put(y, 0, jnp.where(second == 1, row, 0.0))
        put(y, 9, jnp.where(second == 0, row, 0.0))


def place_geometry(near_ref, slab, x, block_ref, second):
    for f in range(4):
        def put(y, z, row, f=f):
            if f < 3:
                row = row + float((x, y, z)[f])
            near_ref[f, slab, y, z] = jnp.broadcast_to(row, (8, SLOTS))

        assemble(lambda at: block_ref[f, at], second, put)
    near_ref[0, slab] = jnp.where(near_ref[3, slab] == 0.0, FAR, near_ref[0, slab])


def row_sums(sums_ref, out_ref):
    for cell in range(16):
        out_ref[cell // 8, cell % 8 : cell % 8 + 1, :] = jnp.sum(sums_ref[cell].T, axis=0, keepdims=True)


def each_cell(one_cell):
    for y in range(2):
        def cell_of(z, _, y=y):
            one_cell(y, z)
            return 0

        lax.fori_loop(0, 8, cell_of, 0)


def weigh(counts_ref, near_ref, mine_ref, weight_refs, old_sums_ref, sums_ref):
    def one_cell(y, z):
        cell = y * 8 + z
        groups = (counts_ref[0, y, z] + 7) >> 3

        def some_groups(first, count):
            spots = [pl.ds(pl.multiple_of((first + g) * 8, 8), 8) for g in range(count)]
            mine = [[mine_ref[cell, f, spot, :] for f in range(4)] for spot in spots]
            if old_sums_ref is None:
                totals = [jnp.zeros((8, SLOTS), jnp.float32) for _ in spots]
            else:
                totals = [old_sums_ref[cell, spot, :] for spot in spots]
            for slab, weight_ref in enumerate(weight_refs):
                for at in range(9):
                    near = [near_ref[f, slab, y + at // 3, z + at % 3] for f in range(4)]
                    for g in range(count):
                        dx, dy, dz = (near[f] - mine[g][f] for f in range(3))
                        square = dx * dx + dy * dy + dz * dz
                        radius = square * lax.rsqrt(jnp.maximum(square, 1e-30))
                        fall = jnp.maximum(1.0 - radius, 0.0)
                        weight = (square * fall) * (fall * fall) / (square + 0.01)
                        weight = weight * (near[3] + mine[g][3])
                        weight_ref[cell, first + g, at] = weight
                        totals[g] = totals[g] + weight
            for g in range(count):
                sums_ref[cell, spots[g], :] = totals[g]

        def four_groups(quad, _):
            some_groups(quad * 4, 4)
            return 0

        lax.fori_loop(0, groups >> 2, four_groups, 0)

        @pl.when((groups & 2) == 2)
        def _():
            some_groups((groups >> 2) * 4, 2)

        @pl.when((groups & 1) == 1)
        def _():
            some_groups(groups - 1, 1)

    each_cell(one_cell)


def centre_kernel(own_ref, mine_ref):
    cell_row = lax.broadcasted_iota(jnp.int32, (16, SLOTS), 0)
    scale = own_ref[3].reshape(16, SLOTS)
    fields = (
        jnp.where(scale == 0.0, -FAR, own_ref[0].reshape(16, SLOTS) + 1.0),
        own_ref[1].reshape(16, SLOTS) + jnp.where(cell_row >= 8, 2.0, 1.0),
        own_ref[2].reshape(16, SLOTS) + (jnp.where(cell_row >= 8, cell_row - 8, cell_row) + 1).astype(jnp.float32),
        scale,
    )
    for f, field in enumerate(fields):
        columns = field.T
        for cell in range(16):
            mine_ref[cell, f] = jnp.broadcast_to(columns[:, cell : cell + 1], (SLOTS, SLOTS))


def middle_weights_kernel(second_ref, counts_ref, mine_ref, block_ref, weight_ref, sums_ref, near_ref):
    place_geometry(near_ref, 0, 1, block_ref, second_ref[0])
    weigh(counts_ref, near_ref, mine_ref, (weight_ref,), None, sums_ref)


def outer_weights_kernel(
    second_ref, counts_ref, before_ref, after_ref, old_sums_ref, mine_ref, live_ref, dirichlet_ref, coarse_hbm,
    weight_a, weight_c, diagonal_ref, inverse_ref, coarse_ref, near_ref, sums_ref, sems,
):
    copies = fetch(((coarse_hbm, coarse_ref),), sems)
    place_geometry(near_ref, 0, 0, before_ref, second_ref[0])
    place_geometry(near_ref, 1, 2, after_ref, second_ref[0])
    weigh(counts_ref, near_ref, mine_ref, (weight_a, weight_c), old_sums_ref, sums_ref)
    row_sums(sums_ref, diagonal_ref)
    live = live_ref[...]
    sums = jnp.where(live == 0.0, 0.0, diagonal_ref[...])
    inverse_ref[...] = live / (dirichlet_ref[...] + sums)
    diagonal_ref[...] = live * dirichlet_ref[...] + sums
    copies[0].wait()


def coarse_lift(values_ref, coarse_ref, basis_ref, part_ref):
    total = jnp.zeros((64, SLOTS), jnp.float32)
    for t in range(128):
        total = total + coarse_ref[:, t * SLOTS : (t + 1) * SLOTS] * values_ref[t : t + 1, :]
    part_ref[...] = jnp.broadcast_to(jnp.sum(total, axis=1, keepdims=True), (64, SLOTS))
    sums = [[jnp.zeros((8, SLOTS), jnp.float32) for _ in range(2)] for _ in range(2)]
    for k in range(64):
        scale = jnp.broadcast_to(part_ref[k : k + 1, :], (8, SLOTS))
        for y in range(2):
            sums[k % 2][y] = sums[k % 2][y] + scale * basis_ref[k, y]
    return jnp.stack([sums[0][y] + sums[1][y] for y in range(2)])


def total_of(gathered_ref, at):
    rows = gathered_ref[pl.ds(1, 128, stride=2), :]
    lane = lax.broadcasted_iota(jnp.int32, rows.shape, 1)
    return jnp.sum(jnp.where(lane == at, rows, 0.0))


def first_smooth_kernel(gathered_ref, coarse_ref, basis_ref, live_ref, residual_ref, inverse_ref, smoothed_ref, part_ref):
    lifted = coarse_lift(gathered_ref, coarse_ref, basis_ref, part_ref)
    smoothed_ref[...] = residual_ref[...] * inverse_ref[...] + live_ref[...] * lifted


def second_smooth_kernel(
    gathered_ref, coefficient_ref, coarse_ref, basis_ref, live_ref, residual_ref, inverse_ref,
    smoothed_ref, image_ref, new_coefficient_ref, new_residual_ref, new_smoothed_ref, part_ref,
):
    step = total_of(gathered_ref, 0) / total_of(gathered_ref, 1)
    new_coefficient_ref[...] = coefficient_ref[...] - step * gathered_ref[pl.ds(0, 128, stride=2), :]
    lifted = coarse_lift(new_coefficient_ref, coarse_ref, basis_ref, part_ref)
    residual = residual_ref[...] - step * image_ref[...]
    new_residual_ref[...] = residual
    new_smoothed_ref[...] = residual * inverse_ref[...] + live_ref[...] * lifted


def third_smooth_kernel(
    gathered_ref, before_ref, coefficient_ref, coarse_ref, basis_ref, live_ref, residual_ref, inverse_ref,
    first_ref, first_image_ref, smoothed_ref, image_ref,
    pressure_ref, new_residual_ref, new_smoothed_ref, direction_ref, payload_ref, values_ref, part_ref,
):
    inner_first, curve_first = total_of(before_ref, 0), total_of(before_ref, 1)
    inner, curve = total_of(gathered_ref, 0), total_of(gathered_ref, 1)
    cross = total_of(gathered_ref, 2) + total_of(gathered_ref, 3)
    step_first = inner_first / curve_first
    ratio = inner / inner_first
    step = inner / (curve + ratio * (cross + ratio * curve_first))
    values_ref[...] = coefficient_ref[...] - step * (
        gathered_ref[pl.ds(0, 128, stride=2), :] + ratio * before_ref[pl.ds(0, 128, stride=2), :]
    )
    lifted = coarse_lift(values_ref, coarse_ref, basis_ref, part_ref)
    direction = smoothed_ref[...] + ratio * first_ref[...]
    direction_ref[...] = direction
    pressure_ref[...] = step_first * first_ref[...] + step * direction
    residual = residual_ref[...] - step * (image_ref[...] + ratio * first_image_ref[...])
    new_residual_ref[...] = residual
    smoothed = residual * inverse_ref[...] + live_ref[...] * lifted
    new_smoothed_ref[...] = smoothed
    payload_ref[...] = inner_row([(residual, smoothed), (residual_ref[...], smoothed_ref[...])])


def place_field(near_ref, slab, block_ref, second):
    def put(y, z, row):
        near_ref[slab, y, z] = jnp.broadcast_to(row, (8, SLOTS))

    assemble(lambda at: block_ref[at], second, put)


def apply_weights(counts_ref, near_ref, weight_refs, old_sums_ref, sums_ref):
    def one_cell(y, z):
        cell = y * 8 + z

        def two_groups(pair, _):
            spots = [pl.ds(pl.multiple_of((pair * 2 + g) * 8, 8), 8) for g in range(2)]
            parts = [[jnp.zeros((8, SLOTS), jnp.float32) for _ in range(3)] for _ in range(2)]
            if old_sums_ref is not None:
                for g in range(2):
                    parts[g][0] = old_sums_ref[cell, spots[g], :]
            for slab, weight_ref in enumerate(weight_refs):
                for at in range(9):
                    near = near_ref[slab, y + at // 3, z + at % 3]
                    for g in range(2):
                        parts[g][at % 3] = parts[g][at % 3] + weight_ref[cell, pair * 2 + g, at] * near
            for g in range(2):
                sums_ref[cell, spots[g], :] = parts[g][0] + parts[g][1] + parts[g][2]
            return 0

        lax.fori_loop(0, (counts_ref[0, y, z] + 15) >> 4, two_groups, 0)

    each_cell(one_cell)


def middle_image_kernel(second_ref, counts_ref, weight_ref, block_ref, sums_ref, near_ref):
    place_field(near_ref, 0, block_ref, second_ref[0])
    apply_weights(counts_ref, near_ref, (weight_ref,), None, sums_ref)


def image_kernel(
    second_ref, counts_ref, weight_a, weight_c, own_ref, before_ref, after_ref, old_sums_ref,
    live_ref, diagonal_ref, residual_ref, basis_ref, *rest,
):
    olds, (image_ref, payload_ref, near_ref, sums_ref, part_ref) = rest[:-5], rest[-5:]
    second = second_ref[0]
    place_field(near_ref, 0, before_ref, second)
    place_field(near_ref, 1, after_ref, second)
    apply_weights(counts_ref, near_ref, (weight_a, weight_c), old_sums_ref, sums_ref)
    row_sums(sums_ref, image_ref)
    own = own_ref[...]
    image = jnp.where(live_ref[...] == 0.0, 0.0, diagonal_ref[...] * own - image_ref[...])
    image_ref[...] = image
    payload_ref[0:1, :] = project(basis_ref, image, part_ref, second)
    pairs = [(residual_ref[...], own), (own, image)]
    if olds:
        first_ref, first_image_ref = olds
        pairs += [(own, first_image_ref[...]), (first_ref[...], image)]
    payload_ref[1:2, :] = inner_row(pairs)


def steps(axis):
    size = lax.axis_size(axis)
    up = [(i, i + 1) for i in range(size - 1)]
    return up, [(j, i) for i, j in up]


def around(field, second, meanwhile=None):
    count = field.shape[0]
    face = call(top_face_kernel, f32(count, 2, SLOTS), [SM, VM])(second, field)
    across = lax.ppermute(face, "gz", [(0, 1), (1, 0)])
    side = f32(count, 2, 8, SLOTS)
    upper, lower = call(side_faces_kernel, (side, side), [VM] * 2)(field, across)
    up, down = steps("gy")
    below = lax.ppermute(upper, "gy", up)
    above = lax.ppermute(lower, "gy", down)
    if meanwhile is not None:
        below, above, meanwhile = lax.optimization_barrier((below, above, meanwhile))
    block = call(block_kernel, f32(count, 5, 8, SLOTS), [VM] * 4)(field, across, below, above)
    up, down = steps("gx")
    return block, lax.ppermute(block, "gx", up), lax.ppermute(block, "gx", down), meanwhile


def gather(payload):
    theirs = lax.ppermute(payload, "gz", [(0, 1), (1, 0)])
    rows = payload.shape[0]
    spread = call(spread_kernel, f32(128, rows, SLOTS), [VM] * 2)(payload, theirs)
    got = lax.all_to_all(spread, ("gx", "gy"), 0, 0, tiled=True)
    return got.reshape(128 * rows, SLOTS)


def per_device(offsets, counts, correction, dirichlet, right_side, deflation, coarse_inverse):
    second = lax.axis_index("gz").astype(jnp.int32)
    second = second.reshape(1)
    block = lambda x: x.reshape(2, 8, SLOTS)
    offsets = offsets.reshape(3, 2, 8, SLOTS)
    dirichlet, right_side, correction = block(dirichlet), block(right_side), block(correction)
    basis = deflation.reshape(64, 2, 8, SLOTS)
    cells = f32(2, 8, SLOTS)

    onchip = lambda x: pltpu.with_memory_space_constraint(x, pltpu.VMEM)
    outside = lambda x: pltpu.with_memory_space_constraint(x, pltpu.HBM)
    vmem = lambda *shape: pltpu.VMEM(shape, jnp.float32)
    part = vmem(64, SLOTS)

    geometry, live, residual, payload, counts, dirichlet, basis = call(
        prepare_kernel,
        (
            f32(4, 2, 8, SLOTS), cells, cells, f32(1, SLOTS),
            pltpu.VMEM((1, 2, 8), jnp.int32), vmem(2, 8, SLOTS), vmem(64, 2, 8, SLOTS),
        ),
        [SM] + [ANY] * 6,
        [
            pltpu.SMEM((1, 2, 8), jnp.int32), vmem(3, 2, 8, SLOTS), vmem(2, 8, SLOTS), vmem(2, 8, SLOTS), part,
            pltpu.SemaphoreType.DMA((7,)),
        ],
    )(second, *map(outside, (counts, offsets, correction, right_side, dirichlet, basis)))
    counts, dirichlet, basis = onchip(counts), onchip(dirichlet), onchip(basis)
    coefficient = gather(payload)
    coefficient, centre = lax.optimization_barrier((coefficient, geometry))
    mine = call(centre_kernel, f32(16, 4, SLOTS, SLOTS), [VM])(centre)
    block, before, after, mine = around(geometry, second, mine)

    sums_shape = f32(16, SLOTS, SLOTS)
    weight_shape = vmem(16, 16, 9, 8, SLOTS)
    weight_b, sums = call(
        middle_weights_kernel,
        (weight_shape, sums_shape),
        [SM, SM] + [VM] * 2,
        [vmem(4, 1, 4, 10, 8, SLOTS)],
    )(second, counts, mine, block)
    weight_a, weight_c, diagonal, inverse, coarse = call(
        outer_weights_kernel,
        (weight_shape, weight_shape, cells, cells, vmem(64, 128 * SLOTS)),
        [SM, SM] + [VM] * 6 + [ANY],
        [vmem(4, 2, 4, 10, 8, SLOTS), vmem(16, SLOTS, SLOTS), pltpu.SemaphoreType.DMA((1,))],
    )(second, counts, before, after, sums, mine, live, dirichlet, outside(coarse_inverse))
    weight_a, weight_b, weight_c, coarse = map(onchip, (weight_a, weight_b, weight_c, coarse))

    def image_of(field, residual, *olds):
        block, before, after = (piece[0] for piece in around(field[None], second)[:3])
        sums = call(middle_image_kernel, sums_shape, [SM, SM] + [VM] * 2, [vmem(1, 4, 10, 8, SLOTS)])(
            second, counts, weight_b, block
        )
        return call(
            image_kernel,
            (cells, f32(2, SLOTS)),
            [SM, SM] + [VM] * (10 + len(olds)),
            [vmem(2, 4, 10, 8, SLOTS), vmem(16, SLOTS, SLOTS), part],
        )(
            second, counts, weight_a, weight_c, field, before, after, sums,
            live, diagonal, residual, basis, *olds,
        )

    smoothed = call(first_smooth_kernel, cells, [VM] * 6, [part])(
        coefficient, coarse, basis, live, residual, inverse
    )
    image, payload = image_of(smoothed, residual)
    gathered_first = gather(payload)
    coefficient, residual, second_smoothed = call(
        second_smooth_kernel, (f32(128, SLOTS), cells, cells), [VM] * 9, [part]
    )(gathered_first, coefficient, coarse, basis, live, residual, inverse, smoothed, image)
    second_image, payload = image_of(second_smoothed, residual, smoothed, image)
    gathered = gather(payload)
    pressure, residual, third_smoothed, direction, payload = call(
        third_smooth_kernel,
        (cells, cells, cells, cells, f32(1, SLOTS)),
        [VM] * 12,
        [pltpu.VMEM((128, SLOTS), jnp.float32), part],
    )(
        gathered, gathered_first, coefficient, coarse, basis, live, residual, inverse,
        smoothed, image, second_smoothed, second_image,
    )
    direction = call(finish_kernel, cells, [VM] * 3)(gather(payload), third_smoothed, direction)
    shape = (1, 2, 8, SLOTS)
    return pressure.reshape(shape), residual.reshape(shape), direction.reshape(shape)


def solution(mesh):
    field = P("gx", "gy", "gz", None)
    in_specs = (
        P(None, "gx", "gy", "gz", None),
        P("gx", "gy", "gz"),
        field,
        field,
        field,
        P(None, "gx", "gy", "gz", None),
        P(("gx", "gy", "gz"), None),
    )
    return jax.shard_map(per_device, mesh=mesh, in_specs=in_specs, out_specs=(field,) * 3, check_vma=False)
```

```python
import jax
import jax.numpy as jnp
from jax import lax
from jax.experimental import pallas as pl
from jax.experimental.pallas import tpu as pltpu
from jax.sharding import PartitionSpec as P

SLOTS = 128
FAR = 1000.0
GX, GY = 32, 4
LIMIT = 4 * 2**20

VM = pl.BlockSpec(memory_space=pltpu.VMEM)
SM = pl.BlockSpec(memory_space=pltpu.SMEM)
ANY = pl.BlockSpec(memory_space=pl.ANY)


def f32(*shape):
    return jax.ShapeDtypeStruct(shape, jnp.float32)


def call(kernel, outs, ins, scratch=(), limit=LIMIT):
    return pl.pallas_call(
        kernel,
        out_shape=outs,
        in_specs=ins,
        out_specs=jax.tree.map(lambda _: VM, outs),
        scratch_shapes=scratch,
        compiler_params=pltpu.CompilerParams(vmem_limit_bytes=limit),
    )


def project(basis_ref, field, part_ref, second):
    for k in range(64):
        prod = basis_ref[k, 0] * field[0] + basis_ref[k, 1] * field[1]
        part_ref[k : k + 1, :] = jnp.sum(prod, axis=0, keepdims=True)
    row = jnp.sum(part_ref[...].T, axis=0, keepdims=True)
    both = jnp.concatenate([row, row], axis=1)
    lane = lax.broadcasted_iota(jnp.int32, (1, SLOTS), 1)
    return jnp.where((lane >= 64) == (second == 1), both, 0.0)


def inner_row(pairs):
    lane = lax.broadcasted_iota(jnp.int32, (1, SLOTS), 1)
    row = jnp.zeros((1, SLOTS), jnp.float32)
    for at, (left, right) in enumerate(pairs):
        total = jnp.sum(left * right)
        row = jnp.where(lane == at, total, row)
    return row


def fetch(pairs, sems):
    copies = [pltpu.make_async_copy(src, dst, sems.at[at]) for at, (src, dst) in enumerate(pairs)]
    for copy in copies:
        copy.start()
    return copies


def prepare_kernel(
    second_ref, counts_hbm, offsets_hbm, correction_hbm, right_hbm, dirichlet_hbm, basis_hbm,
    geometry_ref, live_ref, residual_ref, payload_ref, counts_ref, dirichlet_ref, basis_ref,
    counts_smem, offsets_ref, correction_ref, right_ref, part_ref, sems,
):
    copies = fetch(
        (
            (counts_hbm, counts_smem), (counts_hbm, counts_ref), (offsets_hbm, offsets_ref),
            (correction_hbm, correction_ref), (right_hbm, right_ref), (dirichlet_hbm, dirichlet_ref),
            (basis_hbm, basis_ref),
        ),
        sems,
    )
    for copy in copies[:-1]:
        copy.wait()
    slot = lax.broadcasted_iota(jnp.int32, (1, SLOTS), 1)
    for y in range(2):
        for z in range(8):
            live_ref[y, z : z + 1, :] = jnp.where(slot < counts_smem[0, y, z], 1.0, 0.0)
    live = live_ref[...]
    geometry_ref[0:3] = offsets_ref[...]
    geometry_ref[3] = correction_ref[...] * live * (10.0 / SLOTS)
    residual_ref[...] = right_ref[...] * live
    copies[-1].wait()
    payload_ref[...] = project(basis_ref, residual_ref[...], part_ref, second_ref[0])


def top_face_kernel(second_ref, field_ref, face_ref):
    second = second_ref[0]
    for f in range(field_ref.shape[0]):
        for y in range(2):
            rows = field_ref[f, y]
            face_ref[f, y : y + 1, :] = jnp.where(second == 0, rows[7:8], rows[0:1])


def side_faces_kernel(field_ref, across_ref, up_ref, down_ref):
    for f in range(field_ref.shape[0]):
        for y, ref in enumerate((down_ref, up_ref)):
            ref[f, 0] = field_ref[f, y]
            ref[f, 1] = jnp.broadcast_to(across_ref[f, y : y + 1, :], (8, SLOTS))


def block_kernel(spot_ref, field_ref, across_ref, below_ref, above_ref, block_ref):
    count = field_ref.shape[0]
    for f in range(count):
        sides = [below_ref[f, 0], above_ref[f, 0], below_ref[f, 1, 0:1], above_ref[f, 1, 0:1]]
        if f == 3:
            inside = (spot_ref[0] > 0, spot_ref[0] < GY - 1)
            sides = [jnp.where(inside[at % 2], rows, 0.0) for at, rows in enumerate(sides)]
        block_ref[f, 0] = sides[0]
        block_ref[f, 1] = field_ref[f, 0]
        block_ref[f, 2] = field_ref[f, 1]
        block_ref[f, 3] = sides[1]
        for y, row in enumerate((sides[2], across_ref[f, 0:1], across_ref[f, 1:2], sides[3])):
            block_ref[f, 4, y : y + 1, :] = row


def spread_kernel(mine_ref, theirs_ref, spread_ref):
    rows = mine_ref[...] + theirs_ref[...]
    spread_ref[...] = jnp.broadcast_to(rows[None], spread_ref.shape)


def finish_kernel(
    gathered_ref, smoothed_ref, direction_ref, pressure_ref, residual_ref, pressure_out, residual_out, out_ref
):
    rows = gathered_ref[...]
    lane = lax.broadcasted_iota(jnp.int32, rows.shape, 1)
    inner = jnp.sum(jnp.where(lane == 0, rows, 0.0))
    before = jnp.sum(jnp.where(lane == 1, rows, 0.0))
    out_ref[...] = smoothed_ref[...] + inner / before * direction_ref[...]
    pressure_out[...] = pressure_ref[...]
    residual_out[...] = residual_ref[...]


def assemble(block, second, put):
    for y in range(4):
        rows = block(y)
        for z in range(8):
            put(y, z + 1, rows[z : z + 1])
        row = block(4)[y : y + 1]
        put(y, 0, jnp.where(second == 1, row, 0.0))
        put(y, 9, jnp.where(second == 0, row, 0.0))


def place_geometry(near_ref, slab, x, block_ref, second, inside=None):
    for f in range(4):
        def put(y, z, row, f=f):
            if f < 3:
                row = row + float((x, y, z)[f])
            elif inside is not None:
                row = jnp.where(inside, row, 0.0)
            near_ref[f, slab, y, z] = jnp.broadcast_to(row, (8, SLOTS))

        assemble(lambda at: block_ref[f, at], second, put)
    near_ref[0, slab] = jnp.where(near_ref[3, slab] == 0.0, FAR, near_ref[0, slab])


def row_sums(sums_ref, out_ref):
    for cell in range(16):
        out_ref[cell // 8, cell % 8 : cell % 8 + 1, :] = jnp.sum(sums_ref[cell].T, axis=0, keepdims=True)


def each_cell(one_cell):
    for y in range(2):
        def cell_of(z, _, y=y):
            one_cell(y, z)
            return 0

        lax.fori_loop(0, 8, cell_of, 0)


def weigh(counts_ref, near_ref, mine_ref, weight_refs, old_sums_ref, sums_ref):
    def one_cell(y, z):
        cell = y * 8 + z
        groups = (counts_ref[0, y, z] + 7) >> 3

        def some_groups(first, count):
            spots = [pl.ds(pl.multiple_of((first + g) * 8, 8), 8) for g in range(count)]
            mine = [[mine_ref[cell, f, spot, :] for f in range(4)] for spot in spots]
            if old_sums_ref is None:
                totals = [jnp.zeros((8, SLOTS), jnp.float32) for _ in spots]
            else:
                totals = [old_sums_ref[cell, spot, :] for spot in spots]
            for slab, weight_ref in enumerate(weight_refs):
                for at in range(9):
                    near = [near_ref[f, slab, y + at // 3, z + at % 3] for f in range(4)]
                    for g in range(count):
                        dx, dy, dz = (near[f] - mine[g][f] for f in range(3))
                        square = dx * dx + dy * dy + dz * dz
                        radius = square * lax.rsqrt(jnp.maximum(square, 1e-30))
                        fall = jnp.maximum(1.0 - radius, 0.0)
                        weight = (square * fall) * (fall * fall) / (square + 0.01)
                        weight = weight * (near[3] + mine[g][3])
                        weight_ref[cell, first + g, at] = weight
                        totals[g] = totals[g] + weight
            for g in range(count):
                sums_ref[cell, spots[g], :] = totals[g]

        def four_groups(quad, _):
            some_groups(quad * 4, 4)
            return 0

        lax.fori_loop(0, groups >> 2, four_groups, 0)

        @pl.when((groups & 2) == 2)
        def _():
            some_groups((groups >> 2) * 4, 2)

        @pl.when((groups & 1) == 1)
        def _():
            some_groups(groups - 1, 1)

    each_cell(one_cell)


def centre_kernel(own_ref, mine_ref):
    cell_row = lax.broadcasted_iota(jnp.int32, (16, SLOTS), 0)
    scale = own_ref[3].reshape(16, SLOTS)
    fields = (
        jnp.where(scale == 0.0, -FAR, own_ref[0].reshape(16, SLOTS) + 1.0),
        own_ref[1].reshape(16, SLOTS) + jnp.where(cell_row >= 8, 2.0, 1.0),
        own_ref[2].reshape(16, SLOTS) + (jnp.where(cell_row >= 8, cell_row - 8, cell_row) + 1).astype(jnp.float32),
        scale,
    )
    for f, field in enumerate(fields):
        columns = field.T
        for cell in range(16):
            mine_ref[cell, f] = jnp.broadcast_to(columns[:, cell : cell + 1], (SLOTS, SLOTS))


def middle_weights_kernel(second_ref, counts_ref, mine_ref, block_ref, weight_ref, sums_ref, near_ref):
    place_geometry(near_ref, 0, 1, block_ref, second_ref[0])
    weigh(counts_ref, near_ref, mine_ref, (weight_ref,), None, sums_ref)


def outer_weights_kernel(
    second_ref, spot_ref, counts_ref, before_ref, after_ref, old_sums_ref, mine_ref, live_ref, dirichlet_ref, coarse_hbm,
    weight_a, weight_c, diagonal_ref, inverse_ref, coarse_ref, near_ref, sums_ref, sems,
):
    copies = fetch(((coarse_hbm, coarse_ref),), sems)
    place_geometry(near_ref, 0, 0, before_ref, second_ref[0], spot_ref[0] > 0)
    place_geometry(near_ref, 1, 2, after_ref, second_ref[0], spot_ref[0] < GX - 1)
    weigh(counts_ref, near_ref, mine_ref, (weight_a, weight_c), old_sums_ref, sums_ref)
    row_sums(sums_ref, diagonal_ref)
    live = live_ref[...]
    sums = jnp.where(live == 0.0, 0.0, diagonal_ref[...])
    inverse_ref[...] = live / (dirichlet_ref[...] + sums)
    diagonal_ref[...] = live * dirichlet_ref[...] + sums
    copies[0].wait()


def coarse_lift(values_ref, coarse_ref, basis_ref, part_ref):
    total = jnp.zeros((64, SLOTS), jnp.float32)
    for t in range(128):
        total = total + coarse_ref[:, t * SLOTS : (t + 1) * SLOTS] * values_ref[t : t + 1, :]
    part_ref[...] = jnp.broadcast_to(jnp.sum(total, axis=1, keepdims=True), (64, SLOTS))
    sums = [[jnp.zeros((8, SLOTS), jnp.float32) for _ in range(2)] for _ in range(2)]
    for k in range(64):
        scale = jnp.broadcast_to(part_ref[k : k + 1, :], (8, SLOTS))
        for y in range(2):
            sums[k % 2][y] = sums[k % 2][y] + scale * basis_ref[k, y]
    return jnp.stack([sums[0][y] + sums[1][y] for y in range(2)])


def total_of(gathered_ref, at):
    rows = gathered_ref[pl.ds(1, 128, stride=2), :]
    lane = lax.broadcasted_iota(jnp.int32, rows.shape, 1)
    return jnp.sum(jnp.where(lane == at, rows, 0.0))


def first_smooth_kernel(gathered_ref, coarse_ref, basis_ref, live_ref, residual_ref, inverse_ref, smoothed_ref, part_ref):
    lifted = coarse_lift(gathered_ref, coarse_ref, basis_ref, part_ref)
    smoothed_ref[...] = residual_ref[...] * inverse_ref[...] + live_ref[...] * lifted


def second_smooth_kernel(
    gathered_ref, coefficient_ref, coarse_ref, basis_ref, live_ref, residual_ref, inverse_ref,
    smoothed_ref, image_ref, new_coefficient_ref, new_residual_ref, new_smoothed_ref, part_ref,
):
    step = total_of(gathered_ref, 0) / total_of(gathered_ref, 1)
    new_coefficient_ref[...] = coefficient_ref[...] - step * gathered_ref[pl.ds(0, 128, stride=2), :]
    lifted = coarse_lift(new_coefficient_ref, coarse_ref, basis_ref, part_ref)
    residual = residual_ref[...] - step * image_ref[...]
    new_residual_ref[...] = residual
    new_smoothed_ref[...] = residual * inverse_ref[...] + live_ref[...] * lifted


def third_smooth_kernel(
    gathered_ref, before_ref, coefficient_ref, coarse_ref, basis_ref, live_ref, residual_ref, inverse_ref,
    first_ref, first_image_ref, smoothed_ref, image_ref,
    pressure_ref, new_residual_ref, new_smoothed_ref, direction_ref, payload_ref, values_ref, part_ref,
):
    inner_first, curve_first = total_of(before_ref, 0), total_of(before_ref, 1)
    inner, curve = total_of(gathered_ref, 0), total_of(gathered_ref, 1)
    cross = total_of(gathered_ref, 2) + total_of(gathered_ref, 3)
    step_first = inner_first / curve_first
    ratio = inner / inner_first
    step = inner / (curve + ratio * (cross + ratio * curve_first))
    values_ref[...] = coefficient_ref[...] - step * (
        gathered_ref[pl.ds(0, 128, stride=2), :] + ratio * before_ref[pl.ds(0, 128, stride=2), :]
    )
    lifted = coarse_lift(values_ref, coarse_ref, basis_ref, part_ref)
    direction = smoothed_ref[...] + ratio * first_ref[...]
    direction_ref[...] = direction
    pressure_ref[...] = step_first * first_ref[...] + step * direction
    residual = residual_ref[...] - step * (image_ref[...] + ratio * first_image_ref[...])
    new_residual_ref[...] = residual
    smoothed = residual * inverse_ref[...] + live_ref[...] * lifted
    new_smoothed_ref[...] = smoothed
    payload_ref[...] = inner_row([(residual, smoothed), (residual_ref[...], smoothed_ref[...])])


def place_field(near_ref, slab, block_ref, second):
    def put(y, z, row):
        near_ref[slab, y, z] = jnp.broadcast_to(row, (8, SLOTS))

    assemble(lambda at: block_ref[at], second, put)


def apply_weights(counts_ref, near_ref, weight_refs, old_sums_ref, sums_ref):
    def one_cell(y, z):
        cell = y * 8 + z
        groups = (counts_ref[0, y, z] + 7) >> 3

        def some_groups(first, count):
            spots = [pl.ds(pl.multiple_of((first + g) * 8, 8), 8) for g in range(count)]
            parts = [[jnp.zeros((8, SLOTS), jnp.float32) for _ in range(3)] for _ in range(count)]
            if old_sums_ref is not None:
                for g in range(count):
                    parts[g][0] = old_sums_ref[cell, spots[g], :]
            for slab, weight_ref in enumerate(weight_refs):
                for at in range(9):
                    near = near_ref[slab, y + at // 3, z + at % 3]
                    for g in range(count):
                        parts[g][at % 3] = parts[g][at % 3] + weight_ref[cell, first + g, at] * near
            for g in range(count):
                sums_ref[cell, spots[g], :] = parts[g][0] + parts[g][1] + parts[g][2]

        def four_groups(quad, _):
            some_groups(quad * 4, 4)
            return 0

        def two_groups(pair, _):
            some_groups((groups >> 2) * 4 + pair * 2, 2)
            return 0

        lax.fori_loop(0, groups >> 2, four_groups, 0)
        lax.fori_loop(0, ((groups & 3) + 1) >> 1, two_groups, 0)

    each_cell(one_cell)


def middle_image_kernel(second_ref, counts_ref, weight_ref, block_ref, sums_ref, near_ref):
    place_field(near_ref, 0, block_ref, second_ref[0])
    apply_weights(counts_ref, near_ref, (weight_ref,), None, sums_ref)


def image_kernel(
    second_ref, counts_ref, weight_a, weight_c, own_ref, before_ref, after_ref, old_sums_ref,
    live_ref, diagonal_ref, residual_ref, basis_ref, *rest,
):
    olds, (image_ref, payload_ref, near_ref, sums_ref, part_ref) = rest[:-5], rest[-5:]
    second = second_ref[0]
    place_field(near_ref, 0, before_ref, second)
    place_field(near_ref, 1, after_ref, second)
    apply_weights(counts_ref, near_ref, (weight_a, weight_c), old_sums_ref, sums_ref)
    row_sums(sums_ref, image_ref)
    own = own_ref[...]
    image = jnp.where(live_ref[...] == 0.0, 0.0, diagonal_ref[...] * own - image_ref[...])
    image_ref[...] = image
    payload_ref[0:1, :] = project(basis_ref, image, part_ref, second)
    pairs = [(residual_ref[...], own), (own, image)]
    if olds:
        first_ref, first_image_ref = olds
        pairs += [(own, first_image_ref[...]), (first_ref[...], image)]
    payload_ref[1:2, :] = inner_row(pairs)


def turns(axis):
    size = lax.axis_size(axis)
    up = [(i, (i + 1) % size) for i in range(size)]
    return up, [(j, i) for i, j in up]


def around(field, second, gy_spot):
    count = field.shape[0]
    face = call(top_face_kernel, f32(count, 2, SLOTS), [SM, VM])(second, field)
    across = lax.ppermute(face, "gz", [(0, 1), (1, 0)])
    side = f32(count, 2, 8, SLOTS)
    upper, lower = call(side_faces_kernel, (side, side), [VM] * 2)(field, across)
    up, down = turns("gy")
    below = lax.ppermute(upper, "gy", up)
    above = lax.ppermute(lower, "gy", down)
    block = call(block_kernel, f32(count, 5, 8, SLOTS), [SM] + [VM] * 4)(gy_spot, field, across, below, above)
    up, down = turns("gx")
    return block, lax.ppermute(block, "gx", up), lax.ppermute(block, "gx", down)


def gather(payload):
    theirs = lax.ppermute(payload, "gz", [(0, 1), (1, 0)])
    rows = payload.shape[0]
    spread = call(spread_kernel, f32(128, rows, SLOTS), [VM] * 2)(payload, theirs)
    got = lax.all_to_all(spread, ("gx", "gy"), 0, 0, tiled=True)
    return got.reshape(128 * rows, SLOTS)


def per_device(offsets, counts, correction, dirichlet, right_side, deflation, coarse_inverse):
    second = lax.axis_index("gz").astype(jnp.int32)
    second = second.reshape(1)
    gx_spot, gy_spot = (lax.axis_index(axis).astype(jnp.int32).reshape(1) for axis in ("gx", "gy"))
    block = lambda x: x.reshape(2, 8, SLOTS)
    offsets = offsets.reshape(3, 2, 8, SLOTS)
    dirichlet, right_side, correction = block(dirichlet), block(right_side), block(correction)
    basis = deflation.reshape(64, 2, 8, SLOTS)
    cells = f32(2, 8, SLOTS)

    onchip = lambda x: pltpu.with_memory_space_constraint(x, pltpu.VMEM)
    outside = lambda x: pltpu.with_memory_space_constraint(x, pltpu.HBM)
    vmem = lambda *shape: pltpu.VMEM(shape, jnp.float32)
    part = vmem(64, SLOTS)

    geometry, live, residual, payload, counts, dirichlet, basis = call(
        prepare_kernel,
        (
            f32(4, 2, 8, SLOTS), cells, cells, f32(1, SLOTS),
            pltpu.VMEM((1, 2, 8), jnp.int32), vmem(2, 8, SLOTS), vmem(64, 2, 8, SLOTS),
        ),
        [SM] + [ANY] * 6,
        [
            pltpu.SMEM((1, 2, 8), jnp.int32), vmem(3, 2, 8, SLOTS), vmem(2, 8, SLOTS), vmem(2, 8, SLOTS), part,
            pltpu.SemaphoreType.DMA((7,)),
        ],
    )(second, *map(outside, (counts, offsets, correction, right_side, dirichlet, basis)))
    counts, dirichlet, basis = onchip(counts), onchip(dirichlet), onchip(basis)
    coefficient = gather(payload)
    block, before, after = around(geometry, second, gy_spot)
    coefficient, block, centre = lax.optimization_barrier((coefficient, block, geometry))
    mine = call(centre_kernel, f32(16, 4, SLOTS, SLOTS), [VM])(centre)

    sums_shape = f32(16, SLOTS, SLOTS)
    weight_shape = vmem(16, 16, 9, 8, SLOTS)
    weight_b, sums = call(
        middle_weights_kernel,
        (weight_shape, sums_shape),
        [SM, SM] + [VM] * 2,
        [vmem(4, 1, 4, 10, 8, SLOTS)],
    )(second, counts, mine, block)
    weight_a, weight_c, diagonal, inverse, coarse = call(
        outer_weights_kernel,
        (weight_shape, weight_shape, cells, cells, vmem(64, 128 * SLOTS)),
        [SM, SM, SM] + [VM] * 6 + [ANY],
        [vmem(4, 2, 4, 10, 8, SLOTS), vmem(16, SLOTS, SLOTS), pltpu.SemaphoreType.DMA((1,))],
    )(second, gx_spot, counts, before, after, sums, mine, live, dirichlet, outside(coarse_inverse))
    weight_a, weight_b, weight_c, coarse = map(onchip, (weight_a, weight_b, weight_c, coarse))

    def image_of(field, residual, *olds):
        block, before, after = (piece[0] for piece in around(field[None], second, gy_spot))
        sums = call(middle_image_kernel, sums_shape, [SM, SM] + [VM] * 2, [vmem(1, 4, 10, 8, SLOTS)])(
            second, counts, weight_b, block
        )
        return call(
            image_kernel,
            (cells, f32(2, SLOTS)),
            [SM, SM] + [VM] * (10 + len(olds)),
            [vmem(2, 4, 10, 8, SLOTS), vmem(16, SLOTS, SLOTS), part],
        )(
            second, counts, weight_a, weight_c, field, before, after, sums,
            live, diagonal, residual, basis, *olds,
        )

    smoothed = call(first_smooth_kernel, cells, [VM] * 6, [part])(
        coefficient, coarse, basis, live, residual, inverse
    )
    image, payload = image_of(smoothed, residual)
    gathered_first = gather(payload)
    coefficient, residual, second_smoothed = call(
        second_smooth_kernel, (f32(128, SLOTS), cells, cells), [VM] * 9, [part]
    )(gathered_first, coefficient, coarse, basis, live, residual, inverse, smoothed, image)
    second_image, payload = image_of(second_smoothed, residual, smoothed, image)
    gathered = gather(payload)
    pressure, residual, third_smoothed, direction, payload = call(
        third_smooth_kernel,
        (vmem(2, 8, SLOTS), vmem(2, 8, SLOTS), cells, cells, f32(1, SLOTS)),
        [VM] * 12,
        [pltpu.VMEM((128, SLOTS), jnp.float32), part],
    )(
        gathered, gathered_first, coefficient, coarse, basis, live, residual, inverse,
        smoothed, image, second_smoothed, second_image,
    )
    pressure, residual, direction = call(finish_kernel, (cells, cells, cells), [VM] * 5)(
        gather(payload), third_smoothed, direction, onchip(pressure), onchip(residual)
    )
    shape = (1, 2, 8, SLOTS)
    return pressure.reshape(shape), residual.reshape(shape), direction.reshape(shape)


def solution(mesh):
    field = P("gx", "gy", "gz", None)
    in_specs = (
        P(None, "gx", "gy", "gz", None),
        P("gx", "gy", "gz"),
        field,
        field,
        field,
        P(None, "gx", "gy", "gz", None),
        P(("gx", "gy", "gz"), None),
    )
    return jax.shard_map(per_device, mesh=mesh, in_specs=in_specs, out_specs=(field,) * 3, check_vma=False)
```

```python
import jax
import jax.numpy as jnp
from jax import lax
from jax.experimental import pallas as pl
from jax.experimental.pallas import tpu as pltpu
from jax.sharding import PartitionSpec as P

SLOTS = 128
FAR = 1000.0
GX, GY = 32, 4
LIMIT = 4 * 2**20

VM = pl.BlockSpec(memory_space=pltpu.VMEM)
SM = pl.BlockSpec(memory_space=pltpu.SMEM)
ANY = pl.BlockSpec(memory_space=pl.ANY)


def f32(*shape):
    return jax.ShapeDtypeStruct(shape, jnp.float32)


def call(kernel, outs, ins, scratch=(), limit=LIMIT):
    return pl.pallas_call(
        kernel,
        out_shape=outs,
        in_specs=ins,
        out_specs=jax.tree.map(lambda _: VM, outs),
        scratch_shapes=scratch,
        compiler_params=pltpu.CompilerParams(vmem_limit_bytes=limit),
    )


def project(basis_ref, field, part_ref, second):
    for k in range(64):
        prod = basis_ref[k, 0] * field[0] + basis_ref[k, 1] * field[1]
        part_ref[k : k + 1, :] = jnp.sum(prod, axis=0, keepdims=True)
    row = jnp.sum(part_ref[...].T, axis=0, keepdims=True)
    both = jnp.concatenate([row, row], axis=1)
    lane = lax.broadcasted_iota(jnp.int32, (1, SLOTS), 1)
    return jnp.where((lane >= 64) == (second == 1), both, 0.0)


def inner_row(pairs):
    lane = lax.broadcasted_iota(jnp.int32, (1, SLOTS), 1)
    row = jnp.zeros((1, SLOTS), jnp.float32)
    for at, (left, right) in enumerate(pairs):
        total = jnp.sum(left * right)
        row = jnp.where(lane == at, total, row)
    return row


def fetch(pairs, sems):
    copies = [pltpu.make_async_copy(src, dst, sems.at[at]) for at, (src, dst) in enumerate(pairs)]
    for copy in copies:
        copy.start()
    return copies


def prepare_kernel(
    second_ref, counts_hbm, offsets_hbm, correction_hbm, right_hbm, dirichlet_hbm, basis_hbm,
    geometry_ref, live_ref, residual_ref, payload_ref, counts_ref, dirichlet_ref, basis_ref,
    counts_smem, offsets_ref, correction_ref, right_ref, part_ref, sems,
):
    copies = fetch(
        (
            (counts_hbm, counts_smem), (counts_hbm, counts_ref), (offsets_hbm, offsets_ref),
            (correction_hbm, correction_ref), (right_hbm, right_ref), (dirichlet_hbm, dirichlet_ref),
            (basis_hbm, basis_ref),
        ),
        sems,
    )
    for copy in copies[:-1]:
        copy.wait()
    slot = lax.broadcasted_iota(jnp.int32, (1, SLOTS), 1)
    for y in range(2):
        for z in range(8):
            live_ref[y, z : z + 1, :] = jnp.where(slot < counts_smem[0, y, z], 1.0, 0.0)
    live = live_ref[...]
    geometry_ref[0:3] = offsets_ref[...]
    geometry_ref[3] = correction_ref[...] * live * (10.0 / SLOTS)
    residual_ref[...] = right_ref[...] * live
    copies[-1].wait()
    payload_ref[...] = project(basis_ref, residual_ref[...], part_ref, second_ref[0])


def top_face_kernel(second_ref, field_ref, face_ref):
    second = second_ref[0]
    for f in range(field_ref.shape[0]):
        for y in range(2):
            rows = field_ref[f, y]
            face_ref[f, y : y + 1, :] = jnp.where(second == 0, rows[7:8], rows[0:1])


def side_faces_kernel(field_ref, across_ref, up_ref, down_ref):
    for f in range(field_ref.shape[0]):
        for y, ref in enumerate((down_ref, up_ref)):
            ref[f, 0] = field_ref[f, y]
            ref[f, 1] = jnp.broadcast_to(across_ref[f, y : y + 1, :], (8, SLOTS))


def block_kernel(spot_ref, field_ref, across_ref, below_ref, above_ref, block_ref):
    count = field_ref.shape[0]
    for f in range(count):
        sides = [below_ref[f, 0], above_ref[f, 0], below_ref[f, 1, 0:1], above_ref[f, 1, 0:1]]
        if f == 3:
            inside = (spot_ref[0] > 0, spot_ref[0] < GY - 1)
            sides = [jnp.where(inside[at % 2], rows, 0.0) for at, rows in enumerate(sides)]
        block_ref[f, 0] = sides[0]
        block_ref[f, 1] = field_ref[f, 0]
        block_ref[f, 2] = field_ref[f, 1]
        block_ref[f, 3] = sides[1]
        for y, row in enumerate((sides[2], across_ref[f, 0:1], across_ref[f, 1:2], sides[3])):
            block_ref[f, 4, y : y + 1, :] = row


def spread_kernel(mine_ref, theirs_ref, spread_ref):
    rows = mine_ref[...] + theirs_ref[...]
    spread_ref[...] = jnp.broadcast_to(rows[None], spread_ref.shape)


def finish_kernel(
    gathered_ref, smoothed_ref, direction_ref, pressure_ref, residual_ref, pressure_out, residual_out, out_ref
):
    rows = gathered_ref[...]
    lane = lax.broadcasted_iota(jnp.int32, rows.shape, 1)
    inner = jnp.sum(jnp.where(lane == 0, rows, 0.0))
    before = jnp.sum(jnp.where(lane == 1, rows, 0.0))
    out_ref[...] = smoothed_ref[...] + inner / before * direction_ref[...]
    pressure_out[...] = pressure_ref[...]
    residual_out[...] = residual_ref[...]


def assemble(block, second, put):
    for y in range(4):
        rows = block(y)
        for z in range(8):
            put(y, z + 1, rows[z : z + 1])
        row = block(4)[y : y + 1]
        put(y, 0, jnp.where(second == 1, row, 0.0))
        put(y, 9, jnp.where(second == 0, row, 0.0))


def place_geometry(near_ref, slab, x, block_ref, second, inside=None):
    for f in range(4):
        def put(y, z, row, f=f):
            if f < 3:
                row = row + float((x, y, z)[f])
            elif inside is not None:
                row = jnp.where(inside, row, 0.0)
            near_ref[f, slab, y, z] = jnp.broadcast_to(row, (8, SLOTS))

        assemble(lambda at: block_ref[f, at], second, put)
    near_ref[0, slab] = jnp.where(near_ref[3, slab] == 0.0, FAR, near_ref[0, slab])


def row_sums(sums_ref, out_ref):
    for cell in range(16):
        out_ref[cell // 8, cell % 8 : cell % 8 + 1, :] = jnp.sum(sums_ref[cell].T, axis=0, keepdims=True)


def each_cell(second, one_cell):
    def plane(y, _):
        def inner(z, _):
            one_cell(y, z + 1 - second, 0, 3)
            return 0

        lax.fori_loop(0, 7, inner, 0)
        one_cell(y, second * 7, 1 - second, 2)
        return 0

    lax.fori_loop(0, 2, plane, 0)


def weigh(second, counts_ref, near_ref, mine_ref, weight_refs, old_sums_ref, sums_ref):
    def one_cell(y, z, layer, layers):
        cell = y * 8 + z
        groups = (counts_ref[0, y, z] + 7) >> 3

        def some_groups(first, count):
            spots = [pl.ds(pl.multiple_of((first + g) * 8, 8), 8) for g in range(count)]
            mine = [[mine_ref[cell, f, spot, :] for f in range(4)] for spot in spots]
            if old_sums_ref is None:
                totals = [jnp.zeros((8, SLOTS), jnp.float32) for _ in spots]
            else:
                totals = [old_sums_ref[cell, spot, :] for spot in spots]
            for slab, weight_ref in enumerate(weight_refs):
                for b, c in [(b, layer + c) for b in range(3) for c in range(layers)]:
                    near = [near_ref[f, slab, y + b, z + c] for f in range(4)]
                    for g in range(count):
                        dx, dy, dz = (near[f] - mine[g][f] for f in range(3))
                        square = dx * dx + dy * dy + dz * dz
                        radius = square * lax.rsqrt(jnp.maximum(square, 1e-30))
                        fall = jnp.maximum(1.0 - radius, 0.0)
                        weight = (square * fall) * (fall * fall) / (square + 0.01)
                        weight = weight * (near[3] + mine[g][3])
                        weight_ref[cell, first + g, b * 3 + c] = weight
                        totals[g] = totals[g] + weight
            for g in range(count):
                sums_ref[cell, spots[g], :] = totals[g]

        def four_groups(quad, _):
            some_groups(quad * 4, 4)
            return 0

        lax.fori_loop(0, groups >> 2, four_groups, 0)

        @pl.when((groups & 2) == 2)
        def _():
            some_groups((groups >> 2) * 4, 2)

        @pl.when((groups & 1) == 1)
        def _():
            some_groups(groups - 1, 1)

    each_cell(second, one_cell)


def centre_kernel(own_ref, mine_ref):
    cell_row = lax.broadcasted_iota(jnp.int32, (16, SLOTS), 0)
    scale = own_ref[3].reshape(16, SLOTS)
    fields = (
        jnp.where(scale == 0.0, -FAR, own_ref[0].reshape(16, SLOTS) + 1.0),
        own_ref[1].reshape(16, SLOTS) + jnp.where(cell_row >= 8, 2.0, 1.0),
        own_ref[2].reshape(16, SLOTS) + (jnp.where(cell_row >= 8, cell_row - 8, cell_row) + 1).astype(jnp.float32),
        scale,
    )
    for f, field in enumerate(fields):
        columns = field.T
        for cell in range(16):
            mine_ref[cell, f] = jnp.broadcast_to(columns[:, cell : cell + 1], (SLOTS, SLOTS))


def middle_weights_kernel(second_ref, counts_ref, mine_ref, block_ref, weight_ref, sums_ref, near_ref):
    place_geometry(near_ref, 0, 1, block_ref, second_ref[0])
    weigh(second_ref[0], counts_ref, near_ref, mine_ref, (weight_ref,), None, sums_ref)


def outer_weights_kernel(
    second_ref, spot_ref, counts_ref, before_ref, after_ref, old_sums_ref, mine_ref, live_ref, dirichlet_ref, coarse_hbm,
    weight_a, weight_c, diagonal_ref, inverse_ref, coarse_ref, near_ref, sums_ref, sems,
):
    copies = fetch(((coarse_hbm, coarse_ref),), sems)
    place_geometry(near_ref, 0, 0, before_ref, second_ref[0], spot_ref[0] > 0)
    place_geometry(near_ref, 1, 2, after_ref, second_ref[0], spot_ref[0] < GX - 1)
    weigh(second_ref[0], counts_ref, near_ref, mine_ref, (weight_a, weight_c), old_sums_ref, sums_ref)
    row_sums(sums_ref, diagonal_ref)
    live = live_ref[...]
    sums = jnp.where(live == 0.0, 0.0, diagonal_ref[...])
    inverse_ref[...] = live / (dirichlet_ref[...] + sums)
    diagonal_ref[...] = live * dirichlet_ref[...] + sums
    copies[0].wait()


def coarse_lift(values_ref, coarse_ref, basis_ref, part_ref):
    total = jnp.zeros((64, SLOTS), jnp.float32)
    for t in range(128):
        total = total + coarse_ref[:, t * SLOTS : (t + 1) * SLOTS] * values_ref[t : t + 1, :]
    part_ref[...] = jnp.broadcast_to(jnp.sum(total, axis=1, keepdims=True), (64, SLOTS))
    sums = [[jnp.zeros((8, SLOTS), jnp.float32) for _ in range(2)] for _ in range(2)]
    for k in range(64):
        scale = jnp.broadcast_to(part_ref[k : k + 1, :], (8, SLOTS))
        for y in range(2):
            sums[k % 2][y] = sums[k % 2][y] + scale * basis_ref[k, y]
    return jnp.stack([sums[0][y] + sums[1][y] for y in range(2)])


def total_of(gathered_ref, at):
    rows = gathered_ref[pl.ds(1, 128, stride=2), :]
    lane = lax.broadcasted_iota(jnp.int32, rows.shape, 1)
    return jnp.sum(jnp.where(lane == at, rows, 0.0))


def first_smooth_kernel(gathered_ref, coarse_ref, basis_ref, live_ref, residual_ref, inverse_ref, smoothed_ref, part_ref):
    lifted = coarse_lift(gathered_ref, coarse_ref, basis_ref, part_ref)
    smoothed_ref[...] = residual_ref[...] * inverse_ref[...] + live_ref[...] * lifted


def second_smooth_kernel(
    gathered_ref, coefficient_ref, coarse_ref, basis_ref, live_ref, residual_ref, inverse_ref,
    smoothed_ref, image_ref, new_coefficient_ref, new_residual_ref, new_smoothed_ref, part_ref,
):
    step = total_of(gathered_ref, 0) / total_of(gathered_ref, 1)
    new_coefficient_ref[...] = coefficient_ref[...] - step * gathered_ref[pl.ds(0, 128, stride=2), :]
    lifted = coarse_lift(new_coefficient_ref, coarse_ref, basis_ref, part_ref)
    residual = residual_ref[...] - step * image_ref[...]
    new_residual_ref[...] = residual
    new_smoothed_ref[...] = residual * inverse_ref[...] + live_ref[...] * lifted


def third_smooth_kernel(
    gathered_ref, before_ref, coefficient_ref, coarse_ref, basis_ref, live_ref, residual_ref, inverse_ref,
    first_ref, first_image_ref, smoothed_ref, image_ref,
    pressure_ref, new_residual_ref, new_smoothed_ref, direction_ref, payload_ref, values_ref, part_ref,
):
    inner_first, curve_first = total_of(before_ref, 0), total_of(before_ref, 1)
    inner, curve = total_of(gathered_ref, 0), total_of(gathered_ref, 1)
    cross = total_of(gathered_ref, 2) + total_of(gathered_ref, 3)
    step_first = inner_first / curve_first
    ratio = inner / inner_first
    step = inner / (curve + ratio * (cross + ratio * curve_first))
    values_ref[...] = coefficient_ref[...] - step * (
        gathered_ref[pl.ds(0, 128, stride=2), :] + ratio * before_ref[pl.ds(0, 128, stride=2), :]
    )
    lifted = coarse_lift(values_ref, coarse_ref, basis_ref, part_ref)
    direction = smoothed_ref[...] + ratio * first_ref[...]
    direction_ref[...] = direction
    pressure_ref[...] = step_first * first_ref[...] + step * direction
    residual = residual_ref[...] - step * (image_ref[...] + ratio * first_image_ref[...])
    new_residual_ref[...] = residual
    smoothed = residual * inverse_ref[...] + live_ref[...] * lifted
    new_smoothed_ref[...] = smoothed
    payload_ref[...] = inner_row([(residual, smoothed), (residual_ref[...], smoothed_ref[...])])


def place_field(near_ref, slab, block_ref, second):
    def put(y, z, row):
        near_ref[slab, y, z] = jnp.broadcast_to(row, (8, SLOTS))

    assemble(lambda at: block_ref[at], second, put)


def apply_weights(second, counts_ref, near_ref, weight_refs, old_sums_ref, sums_ref):
    def one_cell(y, z, layer, layers):
        cell = y * 8 + z
        groups = (counts_ref[0, y, z] + 7) >> 3

        def some_groups(first, count):
            spots = [pl.ds(pl.multiple_of((first + g) * 8, 8), 8) for g in range(count)]
            parts = [[jnp.zeros((8, SLOTS), jnp.float32) for _ in range(3)] for _ in range(count)]
            if old_sums_ref is not None:
                for g in range(count):
                    parts[g][0] = old_sums_ref[cell, spots[g], :]
            for slab, weight_ref in enumerate(weight_refs):
                for b, c in [(b, layer + c) for b in range(3) for c in range(layers)]:
                    near = near_ref[slab, y + b, z + c]
                    for g in range(count):
                        parts[g][b] = parts[g][b] + weight_ref[cell, first + g, b * 3 + c] * near
            for g in range(count):
                sums_ref[cell, spots[g], :] = parts[g][0] + parts[g][1] + parts[g][2]

        def four_groups(quad, _):
            some_groups(quad * 4, 4)
            return 0

        def two_groups(pair, _):
            some_groups((groups >> 2) * 4 + pair * 2, 2)
            return 0

        lax.fori_loop(0, groups >> 2, four_groups, 0)
        lax.fori_loop(0, ((groups & 3) + 1) >> 1, two_groups, 0)

    each_cell(second, one_cell)


def middle_image_kernel(second_ref, counts_ref, weight_ref, block_ref, sums_ref, near_ref):
    place_field(near_ref, 0, block_ref, second_ref[0])
    apply_weights(second_ref[0], counts_ref, near_ref, (weight_ref,), None, sums_ref)


def image_kernel(
    second_ref, counts_ref, weight_a, weight_c, own_ref, before_ref, after_ref, old_sums_ref,
    live_ref, diagonal_ref, residual_ref, basis_ref, *rest,
):
    olds, (image_ref, payload_ref, near_ref, sums_ref, part_ref) = rest[:-5], rest[-5:]
    second = second_ref[0]
    place_field(near_ref, 0, before_ref, second)
    place_field(near_ref, 1, after_ref, second)
    apply_weights(second_ref[0], counts_ref, near_ref, (weight_a, weight_c), old_sums_ref, sums_ref)
    row_sums(sums_ref, image_ref)
    own = own_ref[...]
    image = jnp.where(live_ref[...] == 0.0, 0.0, diagonal_ref[...] * own - image_ref[...])
    image_ref[...] = image
    payload_ref[0:1, :] = project(basis_ref, image, part_ref, second)
    pairs = [(residual_ref[...], own), (own, image)]
    if olds:
        first_ref, first_image_ref = olds
        pairs += [(own, first_image_ref[...]), (first_ref[...], image)]
    payload_ref[1:2, :] = inner_row(pairs)


def turns(axis):
    size = lax.axis_size(axis)
    up = [(i, (i + 1) % size) for i in range(size)]
    return up, [(j, i) for i, j in up]


def around(field, second, gy_spot):
    count = field.shape[0]
    face = call(top_face_kernel, f32(count, 2, SLOTS), [SM, VM])(second, field)
    across = lax.ppermute(face, "gz", [(0, 1), (1, 0)])
    side = f32(count, 2, 8, SLOTS)
    upper, lower = call(side_faces_kernel, (side, side), [VM] * 2)(field, across)
    up, down = turns("gy")
    below = lax.ppermute(upper, "gy", up)
    above = lax.ppermute(lower, "gy", down)
    block = call(block_kernel, f32(count, 5, 8, SLOTS), [SM] + [VM] * 4)(gy_spot, field, across, below, above)
    up, down = turns("gx")
    return block, lax.ppermute(block, "gx", up), lax.ppermute(block, "gx", down)


def gather(payload):
    theirs = lax.ppermute(payload, "gz", [(0, 1), (1, 0)])
    rows = payload.shape[0]
    spread = call(spread_kernel, f32(128, rows, SLOTS), [VM] * 2)(payload, theirs)
    got = lax.all_to_all(spread, ("gx", "gy"), 0, 0, tiled=True)
    return got.reshape(128 * rows, SLOTS)


def per_device(offsets, counts, correction, dirichlet, right_side, deflation, coarse_inverse):
    second = lax.axis_index("gz").astype(jnp.int32)
    second = second.reshape(1)
    gx_spot, gy_spot = (lax.axis_index(axis).astype(jnp.int32).reshape(1) for axis in ("gx", "gy"))
    block = lambda x: x.reshape(2, 8, SLOTS)
    offsets = offsets.reshape(3, 2, 8, SLOTS)
    dirichlet, right_side, correction = block(dirichlet), block(right_side), block(correction)
    basis = deflation.reshape(64, 2, 8, SLOTS)
    cells = f32(2, 8, SLOTS)

    onchip = lambda x: pltpu.with_memory_space_constraint(x, pltpu.VMEM)
    outside = lambda x: pltpu.with_memory_space_constraint(x, pltpu.HBM)
    vmem = lambda *shape: pltpu.VMEM(shape, jnp.float32)
    part = vmem(64, SLOTS)

    geometry, live, residual, payload, counts, dirichlet, basis = call(
        prepare_kernel,
        (
            f32(4, 2, 8, SLOTS), cells, cells, f32(1, SLOTS),
            pltpu.VMEM((1, 2, 8), jnp.int32), vmem(2, 8, SLOTS), vmem(64, 2, 8, SLOTS),
        ),
        [SM] + [ANY] * 6,
        [
            pltpu.SMEM((1, 2, 8), jnp.int32), vmem(3, 2, 8, SLOTS), vmem(2, 8, SLOTS), vmem(2, 8, SLOTS), part,
            pltpu.SemaphoreType.DMA((7,)),
        ],
    )(second, *map(outside, (counts, offsets, correction, right_side, dirichlet, basis)))
    counts, dirichlet, basis = onchip(counts), onchip(dirichlet), onchip(basis)
    coefficient = gather(payload)
    block, before, after = around(geometry, second, gy_spot)
    coefficient, block, centre = lax.optimization_barrier((coefficient, block, geometry))
    mine = call(centre_kernel, f32(16, 4, SLOTS, SLOTS), [VM])(centre)

    sums_shape = f32(16, SLOTS, SLOTS)
    weight_shape = vmem(16, 16, 9, 8, SLOTS)
    weight_b, sums = call(
        middle_weights_kernel,
        (weight_shape, sums_shape),
        [SM, SM] + [VM] * 2,
        [vmem(4, 1, 4, 10, 8, SLOTS)],
    )(second, counts, mine, block)
    weight_a, weight_c, diagonal, inverse, coarse = call(
        outer_weights_kernel,
        (weight_shape, weight_shape, cells, cells, vmem(64, 128 * SLOTS)),
        [SM, SM, SM] + [VM] * 6 + [ANY],
        [vmem(4, 2, 4, 10, 8, SLOTS), vmem(16, SLOTS, SLOTS), pltpu.SemaphoreType.DMA((1,))],
    )(second, gx_spot, counts, before, after, sums, mine, live, dirichlet, outside(coarse_inverse))
    weight_a, weight_b, weight_c, coarse = map(onchip, (weight_a, weight_b, weight_c, coarse))

    def image_of(field, residual, *olds):
        block, before, after = (piece[0] for piece in around(field[None], second, gy_spot))
        sums = call(middle_image_kernel, sums_shape, [SM, SM] + [VM] * 2, [vmem(1, 4, 10, 8, SLOTS)])(
            second, counts, weight_b, block
        )
        return call(
            image_kernel,
            (cells, f32(2, SLOTS)),
            [SM, SM] + [VM] * (10 + len(olds)),
            [vmem(2, 4, 10, 8, SLOTS), vmem(16, SLOTS, SLOTS), part],
        )(
            second, counts, weight_a, weight_c, field, before, after, sums,
            live, diagonal, residual, basis, *olds,
        )

    smoothed = call(first_smooth_kernel, cells, [VM] * 6, [part])(
        coefficient, coarse, basis, live, residual, inverse
    )
    image, payload = image_of(smoothed, residual)
    gathered_first = gather(payload)
    coefficient, residual, second_smoothed = call(
        second_smooth_kernel, (f32(128, SLOTS), cells, cells), [VM] * 9, [part]
    )(gathered_first, coefficient, coarse, basis, live, residual, inverse, smoothed, image)
    second_image, payload = image_of(second_smoothed, residual, smoothed, image)
    gathered = gather(payload)
    pressure, residual, third_smoothed, direction, payload = call(
        third_smooth_kernel,
        (vmem(2, 8, SLOTS), vmem(2, 8, SLOTS), cells, cells, f32(1, SLOTS)),
        [VM] * 12,
        [pltpu.VMEM((128, SLOTS), jnp.float32), part],
    )(
        gathered, gathered_first, coefficient, coarse, basis, live, residual, inverse,
        smoothed, image, second_smoothed, second_image,
    )
    pressure, residual, direction = call(finish_kernel, (cells, cells, cells), [VM] * 5)(
        gather(payload), third_smoothed, direction, onchip(pressure), onchip(residual)
    )
    shape = (1, 2, 8, SLOTS)
    return pressure.reshape(shape), residual.reshape(shape), direction.reshape(shape)


def solution(mesh):
    field = P("gx", "gy", "gz", None)
    in_specs = (
        P(None, "gx", "gy", "gz", None),
        P("gx", "gy", "gz"),
        field,
        field,
        field,
        P(None, "gx", "gy", "gz", None),
        P(("gx", "gy", "gz"), None),
    )
    return jax.shard_map(per_device, mesh=mesh, in_specs=in_specs, out_specs=(field,) * 3, check_vma=False)
```

```python
import jax
import jax.numpy as jnp
from jax import lax
from jax.experimental import pallas as pl
from jax.experimental.pallas import tpu as pltpu
from jax.sharding import PartitionSpec as P

SLOTS = 128
FAR = 1000.0
GX, GY = 32, 4
LIMIT = 4 * 2**20

VM = pl.BlockSpec(memory_space=pltpu.VMEM)
SM = pl.BlockSpec(memory_space=pltpu.SMEM)
ANY = pl.BlockSpec(memory_space=pl.ANY)


def f32(*shape):
    return jax.ShapeDtypeStruct(shape, jnp.float32)


def call(kernel, outs, ins, scratch=(), limit=LIMIT):
    return pl.pallas_call(
        kernel,
        out_shape=outs,
        in_specs=ins,
        out_specs=jax.tree.map(lambda _: VM, outs),
        scratch_shapes=scratch,
        compiler_params=pltpu.CompilerParams(vmem_limit_bytes=limit),
    )


def project(basis_ref, field, part_ref, second):
    for k in range(64):
        prod = basis_ref[k, 0] * field[0] + basis_ref[k, 1] * field[1]
        part_ref[k : k + 1, :] = jnp.sum(prod, axis=0, keepdims=True)
    row = jnp.sum(part_ref[...].T, axis=0, keepdims=True)
    both = jnp.concatenate([row, row], axis=1)
    lane = lax.broadcasted_iota(jnp.int32, (1, SLOTS), 1)
    return jnp.where((lane >= 64) == (second == 1), both, 0.0)


def inner_row(pairs):
    lane = lax.broadcasted_iota(jnp.int32, (1, SLOTS), 1)
    row = jnp.zeros((1, SLOTS), jnp.float32)
    for at, (left, right) in enumerate(pairs):
        total = jnp.sum(left * right)
        row = jnp.where(lane == at, total, row)
    return row


def fetch(pairs, sems):
    copies = [pltpu.make_async_copy(src, dst, sems.at[at]) for at, (src, dst) in enumerate(pairs)]
    for copy in copies:
        copy.start()
    return copies


def facing(rows, second):
    return jnp.where(second == 0, rows[7:8], rows[0:1])


def from_across(across_ref, f, y):
    return across_ref[8 + f * 2 + y : 9 + f * 2 + y, :] if across_ref.ndim == 2 else across_ref[f, y : y + 1]


def prepare_kernel(
    second_ref, counts_hbm, offsets_hbm, correction_hbm, right_hbm, dirichlet_hbm, basis_hbm,
    geometry_ref, live_ref, residual_ref, packed_ref, counts_ref, dirichlet_ref, basis_ref,
    counts_smem, offsets_ref, correction_ref, right_ref, part_ref, sems,
):
    copies = fetch(
        (
            (counts_hbm, counts_smem), (counts_hbm, counts_ref), (offsets_hbm, offsets_ref),
            (correction_hbm, correction_ref), (right_hbm, right_ref), (dirichlet_hbm, dirichlet_ref),
            (basis_hbm, basis_ref),
        ),
        sems,
    )
    for copy in copies[:-1]:
        copy.wait()
    slot = lax.broadcasted_iota(jnp.int32, (1, SLOTS), 1)
    for y in range(2):
        for z in range(8):
            live_ref[y, z : z + 1, :] = jnp.where(slot < counts_smem[0, y, z], 1.0, 0.0)
    live = live_ref[...]
    geometry_ref[0:3] = offsets_ref[...]
    geometry_ref[3] = correction_ref[...] * live * (10.0 / SLOTS)
    residual_ref[...] = right_ref[...] * live
    for f in range(4):
        for y in range(2):
            packed_ref[8 + f * 2 + y : 9 + f * 2 + y, :] = facing(geometry_ref[f, y], second_ref[0])
    copies[-1].wait()
    packed_ref[0:8, :] = jnp.broadcast_to(project(basis_ref, residual_ref[...], part_ref, second_ref[0]), (8, SLOTS))


def top_face_kernel(second_ref, field_ref, face_ref):
    second = second_ref[0]
    for f in range(field_ref.shape[0]):
        for y in range(2):
            face_ref[f, y : y + 1, :] = facing(field_ref[f, y], second)


def side_faces_kernel(field_ref, across_ref, up_ref, down_ref):
    for f in range(field_ref.shape[0]):
        for y, ref in enumerate((down_ref, up_ref)):
            ref[f, 0] = field_ref[f, y]
            ref[f, 1] = jnp.broadcast_to(from_across(across_ref, f, y), (8, SLOTS))


def block_kernel(spot_ref, field_ref, across_ref, below_ref, above_ref, block_ref):
    count = field_ref.shape[0]
    for f in range(count):
        sides = [below_ref[f, 0], above_ref[f, 0], below_ref[f, 1, 0:1], above_ref[f, 1, 0:1]]
        if f == 3:
            inside = (spot_ref[0] > 0, spot_ref[0] < GY - 1)
            sides = [jnp.where(inside[at % 2], rows, 0.0) for at, rows in enumerate(sides)]
        block_ref[f, 0] = sides[0]
        block_ref[f, 1] = field_ref[f, 0]
        block_ref[f, 2] = field_ref[f, 1]
        block_ref[f, 3] = sides[1]
        for y, row in enumerate((sides[2], from_across(across_ref, f, 0), from_across(across_ref, f, 1), sides[3])):
            block_ref[f, 4, y : y + 1, :] = row


def spread_kernel(mine_ref, theirs_ref, spread_ref):
    count = spread_ref.shape[1]
    rows = mine_ref[0:count, :] + theirs_ref[0:count, :]
    spread_ref[...] = jnp.broadcast_to(rows[None], spread_ref.shape)


def finish_kernel(
    gathered_ref, smoothed_ref, direction_ref, pressure_ref, residual_ref, pressure_out, residual_out, out_ref
):
    rows = gathered_ref[...]
    lane = lax.broadcasted_iota(jnp.int32, rows.shape, 1)
    inner = jnp.sum(jnp.where(lane == 0, rows, 0.0))
    before = jnp.sum(jnp.where(lane == 1, rows, 0.0))
    out_ref[...] = smoothed_ref[...] + inner / before * direction_ref[...]
    pressure_out[...] = pressure_ref[...]
    residual_out[...] = residual_ref[...]


def assemble(block, second, put):
    for y in range(4):
        rows = block(y)
        for z in range(8):
            put(y, z + 1, rows[z : z + 1])
        row = block(4)[y : y + 1]
        put(y, 0, jnp.where(second == 1, row, 0.0))
        put(y, 9, jnp.where(second == 0, row, 0.0))


def place_geometry(near_ref, slab, x, block_ref, second, inside=None):
    for f in range(4):
        def put(y, z, row, f=f):
            if f < 3:
                row = row + float((x, y, z)[f])
            elif inside is not None:
                row = jnp.where(inside, row, 0.0)
            near_ref[f, slab, y, z] = jnp.broadcast_to(row, (8, SLOTS))

        assemble(lambda at: block_ref[f, at], second, put)
    near_ref[0, slab] = jnp.where(near_ref[3, slab] == 0.0, FAR, near_ref[0, slab])


def row_sums(sums_ref, out_ref):
    for cell in range(16):
        out_ref[cell // 8, cell % 8 : cell % 8 + 1, :] = jnp.sum(sums_ref[cell].T, axis=0, keepdims=True)


def each_cell(second, one_cell):
    def plane(y, _):
        def inner(z, _):
            one_cell(y, z + 1 - second, 0, 3)
            return 0

        lax.fori_loop(0, 7, inner, 0)
        one_cell(y, second * 7, 1 - second, 2)
        return 0

    lax.fori_loop(0, 2, plane, 0)


def weigh(second, counts_ref, near_ref, mine_ref, weight_refs, old_sums_ref, sums_ref):
    def one_cell(y, z, layer, layers):
        cell = y * 8 + z
        groups = (counts_ref[0, y, z] + 7) >> 3

        def some_groups(first, count):
            spots = [pl.ds(pl.multiple_of((first + g) * 8, 8), 8) for g in range(count)]
            mine = [[mine_ref[cell, f, spot, :] for f in range(4)] for spot in spots]
            if old_sums_ref is None:
                totals = [jnp.zeros((8, SLOTS), jnp.float32) for _ in spots]
            else:
                totals = [old_sums_ref[cell, spot, :] for spot in spots]
            for slab, weight_ref in enumerate(weight_refs):
                for b, c in [(b, layer + c) for b in range(3) for c in range(layers)]:
                    near = [near_ref[f, slab, y + b, z + c] for f in range(4)]
                    for g in range(count):
                        dx, dy, dz = (near[f] - mine[g][f] for f in range(3))
                        square = dx * dx + dy * dy + dz * dz
                        radius = square * lax.rsqrt(jnp.maximum(square, 1e-30))
                        fall = jnp.maximum(1.0 - radius, 0.0)
                        weight = (square * fall) * (fall * fall) / (square + 0.01)
                        weight = weight * (near[3] + mine[g][3])
                        weight_ref[cell, first + g, b * 3 + c] = weight
                        totals[g] = totals[g] + weight
            for g in range(count):
                sums_ref[cell, spots[g], :] = totals[g]

        def four_groups(quad, _):
            some_groups(quad * 4, 4)
            return 0

        lax.fori_loop(0, groups >> 2, four_groups, 0)

        @pl.when((groups & 2) == 2)
        def _():
            some_groups((groups >> 2) * 4, 2)

        @pl.when((groups & 1) == 1)
        def _():
            some_groups(groups - 1, 1)

    each_cell(second, one_cell)


def centre_kernel(own_ref, mine_ref):
    cell_row = lax.broadcasted_iota(jnp.int32, (16, SLOTS), 0)
    scale = own_ref[3].reshape(16, SLOTS)
    fields = (
        jnp.where(scale == 0.0, -FAR, own_ref[0].reshape(16, SLOTS) + 1.0),
        own_ref[1].reshape(16, SLOTS) + jnp.where(cell_row >= 8, 2.0, 1.0),
        own_ref[2].reshape(16, SLOTS) + (jnp.where(cell_row >= 8, cell_row - 8, cell_row) + 1).astype(jnp.float32),
        scale,
    )
    for f, field in enumerate(fields):
        columns = field.T
        for cell in range(16):
            mine_ref[cell, f] = jnp.broadcast_to(columns[:, cell : cell + 1], (SLOTS, SLOTS))


def middle_weights_kernel(second_ref, counts_ref, mine_ref, block_ref, weight_ref, sums_ref, near_ref):
    place_geometry(near_ref, 0, 1, block_ref, second_ref[0])
    weigh(second_ref[0], counts_ref, near_ref, mine_ref, (weight_ref,), None, sums_ref)


def outer_weights_kernel(
    second_ref, spot_ref, counts_ref, before_ref, after_ref, old_sums_ref, mine_ref, live_ref, dirichlet_ref, coarse_hbm,
    weight_a, weight_c, diagonal_ref, inverse_ref, coarse_ref, near_ref, sums_ref, sems,
):
    copies = fetch(((coarse_hbm, coarse_ref),), sems)
    place_geometry(near_ref, 0, 0, before_ref, second_ref[0], spot_ref[0] > 0)
    place_geometry(near_ref, 1, 2, after_ref, second_ref[0], spot_ref[0] < GX - 1)
    weigh(second_ref[0], counts_ref, near_ref, mine_ref, (weight_a, weight_c), old_sums_ref, sums_ref)
    row_sums(sums_ref, diagonal_ref)
    live = live_ref[...]
    sums = jnp.where(live == 0.0, 0.0, diagonal_ref[...])
    inverse_ref[...] = live / (dirichlet_ref[...] + sums)
    diagonal_ref[...] = live * dirichlet_ref[...] + sums
    copies[0].wait()


def coarse_lift(values_ref, coarse_ref, basis_ref, part_ref):
    total = jnp.zeros((64, SLOTS), jnp.float32)
    for t in range(128):
        total = total + coarse_ref[:, t * SLOTS : (t + 1) * SLOTS] * values_ref[t : t + 1, :]
    part_ref[...] = jnp.broadcast_to(jnp.sum(total, axis=1, keepdims=True), (64, SLOTS))
    sums = [[jnp.zeros((8, SLOTS), jnp.float32) for _ in range(2)] for _ in range(2)]
    for k in range(64):
        scale = jnp.broadcast_to(part_ref[k : k + 1, :], (8, SLOTS))
        for y in range(2):
            sums[k % 2][y] = sums[k % 2][y] + scale * basis_ref[k, y]
    return jnp.stack([sums[0][y] + sums[1][y] for y in range(2)])


def total_of(gathered_ref, at):
    rows = gathered_ref[pl.ds(1, 128, stride=2), :]
    lane = lax.broadcasted_iota(jnp.int32, rows.shape, 1)
    return jnp.sum(jnp.where(lane == at, rows, 0.0))


def first_smooth_kernel(gathered_ref, coarse_ref, basis_ref, live_ref, residual_ref, inverse_ref, smoothed_ref, part_ref):
    lifted = coarse_lift(gathered_ref, coarse_ref, basis_ref, part_ref)
    smoothed_ref[...] = residual_ref[...] * inverse_ref[...] + live_ref[...] * lifted


def second_smooth_kernel(
    gathered_ref, coefficient_ref, coarse_ref, basis_ref, live_ref, residual_ref, inverse_ref,
    smoothed_ref, image_ref, new_coefficient_ref, new_residual_ref, new_smoothed_ref, part_ref,
):
    step = total_of(gathered_ref, 0) / total_of(gathered_ref, 1)
    new_coefficient_ref[...] = coefficient_ref[...] - step * gathered_ref[pl.ds(0, 128, stride=2), :]
    lifted = coarse_lift(new_coefficient_ref, coarse_ref, basis_ref, part_ref)
    residual = residual_ref[...] - step * image_ref[...]
    new_residual_ref[...] = residual
    new_smoothed_ref[...] = residual * inverse_ref[...] + live_ref[...] * lifted


def third_smooth_kernel(
    gathered_ref, before_ref, coefficient_ref, coarse_ref, basis_ref, live_ref, residual_ref, inverse_ref,
    first_ref, first_image_ref, smoothed_ref, image_ref,
    pressure_ref, new_residual_ref, new_smoothed_ref, direction_ref, payload_ref, values_ref, part_ref,
):
    inner_first, curve_first = total_of(before_ref, 0), total_of(before_ref, 1)
    inner, curve = total_of(gathered_ref, 0), total_of(gathered_ref, 1)
    cross = total_of(gathered_ref, 2) + total_of(gathered_ref, 3)
    step_first = inner_first / curve_first
    ratio = inner / inner_first
    step = inner / (curve + ratio * (cross + ratio * curve_first))
    values_ref[...] = coefficient_ref[...] - step * (
        gathered_ref[pl.ds(0, 128, stride=2), :] + ratio * before_ref[pl.ds(0, 128, stride=2), :]
    )
    lifted = coarse_lift(values_ref, coarse_ref, basis_ref, part_ref)
    direction = smoothed_ref[...] + ratio * first_ref[...]
    direction_ref[...] = direction
    pressure_ref[...] = step_first * first_ref[...] + step * direction
    residual = residual_ref[...] - step * (image_ref[...] + ratio * first_image_ref[...])
    new_residual_ref[...] = residual
    smoothed = residual * inverse_ref[...] + live_ref[...] * lifted
    new_smoothed_ref[...] = smoothed
    payload_ref[...] = inner_row([(residual, smoothed), (residual_ref[...], smoothed_ref[...])])


def place_field(near_ref, slab, block_ref, second):
    def put(y, z, row):
        near_ref[slab, y, z] = jnp.broadcast_to(row, (8, SLOTS))

    assemble(lambda at: block_ref[at], second, put)


def apply_weights(second, counts_ref, near_ref, weight_refs, old_sums_ref, sums_ref):
    def one_cell(y, z, layer, layers):
        cell = y * 8 + z
        groups = (counts_ref[0, y, z] + 7) >> 3

        def some_groups(first, count):
            spots = [pl.ds(pl.multiple_of((first + g) * 8, 8), 8) for g in range(count)]
            parts = [[jnp.zeros((8, SLOTS), jnp.float32) for _ in range(3)] for _ in range(count)]
            if old_sums_ref is not None:
                for g in range(count):
                    parts[g][0] = old_sums_ref[cell, spots[g], :]
            for slab, weight_ref in enumerate(weight_refs):
                for b, c in [(b, layer + c) for b in range(3) for c in range(layers)]:
                    near = near_ref[slab, y + b, z + c]
                    for g in range(count):
                        parts[g][b] = parts[g][b] + weight_ref[cell, first + g, b * 3 + c] * near
            for g in range(count):
                sums_ref[cell, spots[g], :] = parts[g][0] + parts[g][1] + parts[g][2]

        def four_groups(quad, _):
            some_groups(quad * 4, 4)
            return 0

        def two_groups(pair, _):
            some_groups((groups >> 2) * 4 + pair * 2, 2)
            return 0

        lax.fori_loop(0, groups >> 2, four_groups, 0)
        lax.fori_loop(0, ((groups & 3) + 1) >> 1, two_groups, 0)

    each_cell(second, one_cell)


def middle_image_kernel(second_ref, counts_ref, weight_ref, block_ref, sums_ref, near_ref):
    place_field(near_ref, 0, block_ref, second_ref[0])
    apply_weights(second_ref[0], counts_ref, near_ref, (weight_ref,), None, sums_ref)


def image_kernel(
    second_ref, counts_ref, weight_a, weight_c, own_ref, before_ref, after_ref, old_sums_ref,
    live_ref, diagonal_ref, residual_ref, basis_ref, *rest,
):
    olds, (image_ref, payload_ref, near_ref, sums_ref, part_ref) = rest[:-5], rest[-5:]
    second = second_ref[0]
    place_field(near_ref, 0, before_ref, second)
    place_field(near_ref, 1, after_ref, second)
    apply_weights(second_ref[0], counts_ref, near_ref, (weight_a, weight_c), old_sums_ref, sums_ref)
    row_sums(sums_ref, image_ref)
    own = own_ref[...]
    image = jnp.where(live_ref[...] == 0.0, 0.0, diagonal_ref[...] * own - image_ref[...])
    image_ref[...] = image
    payload_ref[0:1, :] = project(basis_ref, image, part_ref, second)
    pairs = [(residual_ref[...], own), (own, image)]
    if olds:
        first_ref, first_image_ref = olds
        pairs += [(own, first_image_ref[...]), (first_ref[...], image)]
    payload_ref[1:2, :] = inner_row(pairs)


def swap(x):
    return lax.ppermute(x, "gz", [(0, 1), (1, 0)])


def turns(axis):
    size = lax.axis_size(axis)
    up = [(i, (i + 1) % size) for i in range(size)]
    return up, [(j, i) for i, j in up]


def around(field, second, gy_spot, across=None):
    count = field.shape[0]
    if across is None:
        across = swap(call(top_face_kernel, f32(count, 2, SLOTS), [SM, VM])(second, field))
    side = f32(count, 2, 8, SLOTS)
    upper, lower = call(side_faces_kernel, (side, side), [VM] * 2)(field, across)
    up, down = turns("gy")
    below = lax.ppermute(upper, "gy", up)
    above = lax.ppermute(lower, "gy", down)
    block = call(block_kernel, f32(count, 5, 8, SLOTS), [SM] + [VM] * 4)(gy_spot, field, across, below, above)
    up, down = turns("gx")
    return block, lax.ppermute(block, "gx", up), lax.ppermute(block, "gx", down)


def gather(payload, theirs=None, rows=None):
    theirs = swap(payload) if theirs is None else theirs
    rows = payload.shape[0] if rows is None else rows
    spread = call(spread_kernel, f32(128, rows, SLOTS), [VM] * 2)(payload, theirs)
    got = lax.all_to_all(spread, ("gx", "gy"), 0, 0, tiled=True)
    return got.reshape(128 * rows, SLOTS)


def per_device(offsets, counts, correction, dirichlet, right_side, deflation, coarse_inverse):
    second = lax.axis_index("gz").astype(jnp.int32)
    second = second.reshape(1)
    gx_spot, gy_spot = (lax.axis_index(axis).astype(jnp.int32).reshape(1) for axis in ("gx", "gy"))
    block = lambda x: x.reshape(2, 8, SLOTS)
    offsets = offsets.reshape(3, 2, 8, SLOTS)
    dirichlet, right_side, correction = block(dirichlet), block(right_side), block(correction)
    basis = deflation.reshape(64, 2, 8, SLOTS)
    cells = f32(2, 8, SLOTS)

    onchip = lambda x: pltpu.with_memory_space_constraint(x, pltpu.VMEM)
    outside = lambda x: pltpu.with_memory_space_constraint(x, pltpu.HBM)
    vmem = lambda *shape: pltpu.VMEM(shape, jnp.float32)
    part = vmem(64, SLOTS)

    geometry, live, residual, packed, counts, dirichlet, basis = call(
        prepare_kernel,
        (
            f32(4, 2, 8, SLOTS), cells, cells, f32(16, SLOTS),
            pltpu.VMEM((1, 2, 8), jnp.int32), vmem(2, 8, SLOTS), vmem(64, 2, 8, SLOTS),
        ),
        [SM] + [ANY] * 6,
        [
            pltpu.SMEM((1, 2, 8), jnp.int32), vmem(3, 2, 8, SLOTS), vmem(2, 8, SLOTS), vmem(2, 8, SLOTS), part,
            pltpu.SemaphoreType.DMA((7,)),
        ],
    )(second, *map(outside, (counts, offsets, correction, right_side, dirichlet, basis)))
    counts, dirichlet, basis = onchip(counts), onchip(dirichlet), onchip(basis)
    theirs = swap(packed)
    coefficient = gather(packed, theirs, 1)
    block, before, after = around(geometry, second, gy_spot, theirs)
    coefficient, block, centre = lax.optimization_barrier((coefficient, block, geometry))
    mine = call(centre_kernel, f32(16, 4, SLOTS, SLOTS), [VM])(centre)

    sums_shape = f32(16, SLOTS, SLOTS)
    weight_shape = vmem(16, 16, 9, 8, SLOTS)
    weight_b, sums = call(
        middle_weights_kernel,
        (weight_shape, sums_shape),
        [SM, SM] + [VM] * 2,
        [vmem(4, 1, 4, 10, 8, SLOTS)],
    )(second, counts, mine, block)
    weight_a, weight_c, diagonal, inverse, coarse = call(
        outer_weights_kernel,
        (weight_shape, weight_shape, cells, cells, vmem(64, 128 * SLOTS)),
        [SM, SM, SM] + [VM] * 6 + [ANY],
        [vmem(4, 2, 4, 10, 8, SLOTS), vmem(16, SLOTS, SLOTS), pltpu.SemaphoreType.DMA((1,))],
    )(second, gx_spot, counts, before, after, sums, mine, live, dirichlet, outside(coarse_inverse))
    weight_a, weight_b, weight_c, coarse = map(onchip, (weight_a, weight_b, weight_c, coarse))

    def image_of(field, residual, *olds):
        block, before, after = (piece[0] for piece in around(field[None], second, gy_spot))
        sums = call(middle_image_kernel, sums_shape, [SM, SM] + [VM] * 2, [vmem(1, 4, 10, 8, SLOTS)])(
            second, counts, weight_b, block
        )
        return call(
            image_kernel,
            (cells, f32(2, SLOTS)),
            [SM, SM] + [VM] * (10 + len(olds)),
            [vmem(2, 4, 10, 8, SLOTS), vmem(16, SLOTS, SLOTS), part],
        )(
            second, counts, weight_a, weight_c, field, before, after, sums,
            live, diagonal, residual, basis, *olds,
        )

    smoothed = call(first_smooth_kernel, cells, [VM] * 6, [part])(
        coefficient, coarse, basis, live, residual, inverse
    )
    image, payload = image_of(smoothed, residual)
    gathered_first = gather(payload)
    coefficient, residual, second_smoothed = call(
        second_smooth_kernel, (f32(128, SLOTS), cells, cells), [VM] * 9, [part]
    )(gathered_first, coefficient, coarse, basis, live, residual, inverse, smoothed, image)
    second_image, payload = image_of(second_smoothed, residual, smoothed, image)
    gathered = gather(payload)
    pressure, residual, third_smoothed, direction, payload = call(
        third_smooth_kernel,
        (vmem(2, 8, SLOTS), vmem(2, 8, SLOTS), cells, cells, f32(1, SLOTS)),
        [VM] * 12,
        [pltpu.VMEM((128, SLOTS), jnp.float32), part],
    )(
        gathered, gathered_first, coefficient, coarse, basis, live, residual, inverse,
        smoothed, image, second_smoothed, second_image,
    )
    pressure, residual, direction = call(finish_kernel, (cells, cells, cells), [VM] * 5)(
        gather(payload), third_smoothed, direction, onchip(pressure), onchip(residual)
    )
    shape = (1, 2, 8, SLOTS)
    return pressure.reshape(shape), residual.reshape(shape), direction.reshape(shape)


def solution(mesh):
    field = P("gx", "gy", "gz", None)
    in_specs = (
        P(None, "gx", "gy", "gz", None),
        P("gx", "gy", "gz"),
        field,
        field,
        field,
        P(None, "gx", "gy", "gz", None),
        P(("gx", "gy", "gz"), None),
    )
    return jax.shard_map(per_device, mesh=mesh, in_specs=in_specs, out_specs=(field,) * 3, check_vma=False)
```

```python
import jax
import jax.numpy as jnp
from jax import lax
from jax.experimental import pallas as pl
from jax.experimental.pallas import tpu as pltpu
from jax.sharding import PartitionSpec as P

SLOTS = 128
FAR = 1000.0
GX, GY = 32, 4
LIMIT = 4 * 2**20

VM = pl.BlockSpec(memory_space=pltpu.VMEM)
SM = pl.BlockSpec(memory_space=pltpu.SMEM)
ANY = pl.BlockSpec(memory_space=pl.ANY)


def f32(*shape):
    return jax.ShapeDtypeStruct(shape, jnp.float32)


def call(kernel, outs, ins, scratch=(), limit=LIMIT):
    return pl.pallas_call(
        kernel,
        out_shape=outs,
        in_specs=ins,
        out_specs=jax.tree.map(lambda _: VM, outs),
        scratch_shapes=scratch,
        compiler_params=pltpu.CompilerParams(vmem_limit_bytes=limit),
    )


def project(basis_ref, field, part_ref, second):
    for k in range(64):
        prod = basis_ref[k, 0] * field[0] + basis_ref[k, 1] * field[1]
        part_ref[k : k + 1, :] = jnp.sum(prod, axis=0, keepdims=True)
    row = jnp.sum(part_ref[...].T, axis=0, keepdims=True)
    both = jnp.concatenate([row, row], axis=1)
    lane = lax.broadcasted_iota(jnp.int32, (1, SLOTS), 1)
    return jnp.where((lane >= 64) == (second == 1), both, 0.0)


def inner_row(pairs):
    lane = lax.broadcasted_iota(jnp.int32, (1, SLOTS), 1)
    row = jnp.zeros((1, SLOTS), jnp.float32)
    for at, (left, right) in enumerate(pairs):
        total = jnp.sum(left * right)
        row = jnp.where(lane == at, total, row)
    return row


def fetch(pairs, sems):
    copies = [pltpu.make_async_copy(src, dst, sems.at[at]) for at, (src, dst) in enumerate(pairs)]
    for copy in copies:
        copy.start()
    return copies


def facing(rows, second):
    return jnp.where(second == 0, rows[7:8], rows[0:1])


def from_across(across_ref, f, y):
    return across_ref[8 + f * 2 + y : 9 + f * 2 + y, :] if across_ref.ndim == 2 else across_ref[f, y : y + 1]


def prepare_kernel(
    second_ref, counts_hbm, offsets_hbm, correction_hbm, right_hbm, dirichlet_hbm, basis_hbm,
    geometry_ref, live_ref, residual_ref, packed_ref, counts_ref, dirichlet_ref, basis_ref,
    counts_smem, offsets_ref, correction_ref, right_ref, part_ref, sems,
):
    copies = fetch(
        (
            (counts_hbm, counts_smem), (counts_hbm, counts_ref), (offsets_hbm, offsets_ref),
            (correction_hbm, correction_ref), (right_hbm, right_ref), (dirichlet_hbm, dirichlet_ref),
            (basis_hbm, basis_ref),
        ),
        sems,
    )
    for copy in copies[:-1]:
        copy.wait()
    slot = lax.broadcasted_iota(jnp.int32, (1, SLOTS), 1)
    for y in range(2):
        for z in range(8):
            live_ref[y, z : z + 1, :] = jnp.where(slot < counts_smem[0, y, z], 1.0, 0.0)
    live = live_ref[...]
    geometry_ref[0:3] = offsets_ref[...]
    geometry_ref[3] = correction_ref[...] * live * (10.0 / SLOTS)
    residual_ref[...] = right_ref[...] * live
    for f in range(4):
        for y in range(2):
            packed_ref[8 + f * 2 + y : 9 + f * 2 + y, :] = facing(geometry_ref[f, y], second_ref[0])
    copies[-1].wait()
    packed_ref[0:8, :] = jnp.broadcast_to(project(basis_ref, residual_ref[...], part_ref, second_ref[0]), (8, SLOTS))


def put_face(face_ref, field, second):
    for y in range(2):
        face_ref[0, y : y + 1, :] = facing(field[y], second)


def side_faces_kernel(field_ref, across_ref, up_ref, down_ref):
    for f in range(field_ref.shape[0]):
        for y, ref in enumerate((down_ref, up_ref)):
            ref[f, 0] = field_ref[f, y]
            ref[f, 1] = jnp.broadcast_to(from_across(across_ref, f, y), (8, SLOTS))


def block_kernel(spot_ref, field_ref, across_ref, below_ref, above_ref, block_ref):
    count = field_ref.shape[0]
    for f in range(count):
        sides = [below_ref[f, 0], above_ref[f, 0], below_ref[f, 1, 0:1], above_ref[f, 1, 0:1]]
        if f == 3:
            inside = (spot_ref[0] > 0, spot_ref[0] < GY - 1)
            sides = [jnp.where(inside[at % 2], rows, 0.0) for at, rows in enumerate(sides)]
        block_ref[f, 0] = sides[0]
        block_ref[f, 1] = field_ref[f, 0]
        block_ref[f, 2] = field_ref[f, 1]
        block_ref[f, 3] = sides[1]
        for y, row in enumerate((sides[2], from_across(across_ref, f, 0), from_across(across_ref, f, 1), sides[3])):
            block_ref[f, 4, y : y + 1, :] = row


def spread_kernel(mine_ref, theirs_ref, spread_ref):
    count = spread_ref.shape[1]
    rows = mine_ref[0:count, :] + theirs_ref[0:count, :]
    spread_ref[...] = jnp.broadcast_to(rows[None], spread_ref.shape)


def finish_kernel(
    gathered_ref, smoothed_ref, direction_ref, pressure_ref, residual_ref, pressure_out, residual_out, out_ref
):
    rows = gathered_ref[...]
    lane = lax.broadcasted_iota(jnp.int32, rows.shape, 1)
    inner = jnp.sum(jnp.where(lane == 0, rows, 0.0))
    before = jnp.sum(jnp.where(lane == 1, rows, 0.0))
    out_ref[...] = smoothed_ref[...] + inner / before * direction_ref[...]
    pressure_out[...] = pressure_ref[...]
    residual_out[...] = residual_ref[...]


def assemble(block, second, put):
    for y in range(4):
        rows = block(y)
        for z in range(8):
            put(y, z + 1, rows[z : z + 1])
        row = block(4)[y : y + 1]
        put(y, 0, jnp.where(second == 1, row, 0.0))
        put(y, 9, jnp.where(second == 0, row, 0.0))


def place_geometry(near_ref, slab, x, block_ref, second, inside=None):
    for f in range(4):
        def put(y, z, row, f=f):
            if f < 3:
                row = row + float((x, y, z)[f])
            elif inside is not None:
                row = jnp.where(inside, row, 0.0)
            near_ref[f, slab, y, z] = jnp.broadcast_to(row, (8, SLOTS))

        assemble(lambda at: block_ref[f, at], second, put)
    near_ref[0, slab] = jnp.where(near_ref[3, slab] == 0.0, FAR, near_ref[0, slab])


def row_sums(sums_ref, out_ref):
    for cell in range(16):
        out_ref[cell // 8, cell % 8 : cell % 8 + 1, :] = jnp.sum(sums_ref[cell].T, axis=0, keepdims=True)


def each_cell(second, one_cell):
    def plane(y, _):
        def inner(z, _):
            one_cell(y, z + 1 - second, 0, 3)
            return 0

        lax.fori_loop(0, 7, inner, 0)
        one_cell(y, second * 7, 1 - second, 2)
        return 0

    lax.fori_loop(0, 2, plane, 0)


def weigh(second, counts_ref, near_ref, mine_ref, weight_refs, old_sums_ref, sums_ref):
    def one_cell(y, z, layer, layers):
        cell = y * 8 + z
        groups = (counts_ref[0, y, z] + 7) >> 3

        def some_groups(first, count):
            spots = [pl.ds(pl.multiple_of((first + g) * 8, 8), 8) for g in range(count)]
            mine = [[mine_ref[cell, f, spot, :] for f in range(4)] for spot in spots]
            if old_sums_ref is None:
                totals = [jnp.zeros((8, SLOTS), jnp.float32) for _ in spots]
            else:
                totals = [old_sums_ref[cell, spot, :] for spot in spots]
            for slab, weight_ref in enumerate(weight_refs):
                for b, c in [(b, layer + c) for b in range(3) for c in range(layers)]:
                    near = [near_ref[f, slab, y + b, z + c] for f in range(4)]
                    for g in range(count):
                        dx, dy, dz = (near[f] - mine[g][f] for f in range(3))
                        square = dx * dx + dy * dy + dz * dz
                        radius = square * lax.rsqrt(jnp.maximum(square, 1e-30))
                        fall = jnp.maximum(1.0 - radius, 0.0)
                        weight = (square * fall) * (fall * fall) / (square + 0.01)
                        weight = weight * (near[3] + mine[g][3])
                        weight_ref[cell, first + g, b * 3 + c] = weight
                        totals[g] = totals[g] + weight
            for g in range(count):
                sums_ref[cell, spots[g], :] = totals[g]

        def four_groups(quad, _):
            some_groups(quad * 4, 4)
            return 0

        lax.fori_loop(0, groups >> 2, four_groups, 0)

        @pl.when((groups & 2) == 2)
        def _():
            some_groups((groups >> 2) * 4, 2)

        @pl.when((groups & 1) == 1)
        def _():
            some_groups(groups - 1, 1)

    each_cell(second, one_cell)


def centre_kernel(own_ref, mine_ref):
    cell_row = lax.broadcasted_iota(jnp.int32, (16, SLOTS), 0)
    scale = own_ref[3].reshape(16, SLOTS)
    fields = (
        jnp.where(scale == 0.0, -FAR, own_ref[0].reshape(16, SLOTS) + 1.0),
        own_ref[1].reshape(16, SLOTS) + jnp.where(cell_row >= 8, 2.0, 1.0),
        own_ref[2].reshape(16, SLOTS) + (jnp.where(cell_row >= 8, cell_row - 8, cell_row) + 1).astype(jnp.float32),
        scale,
    )
    for f, field in enumerate(fields):
        columns = field.T
        for cell in range(16):
            mine_ref[cell, f] = jnp.broadcast_to(columns[:, cell : cell + 1], (SLOTS, SLOTS))


def middle_weights_kernel(second_ref, counts_ref, mine_ref, block_ref, weight_ref, sums_ref, near_ref):
    place_geometry(near_ref, 0, 1, block_ref, second_ref[0])
    weigh(second_ref[0], counts_ref, near_ref, mine_ref, (weight_ref,), None, sums_ref)


def outer_weights_kernel(
    second_ref, spot_ref, counts_ref, before_ref, after_ref, old_sums_ref, mine_ref, live_ref, dirichlet_ref, coarse_hbm,
    weight_a, weight_c, diagonal_ref, inverse_ref, coarse_ref, near_ref, sums_ref, sems,
):
    copies = fetch(((coarse_hbm, coarse_ref),), sems)
    place_geometry(near_ref, 0, 0, before_ref, second_ref[0], spot_ref[0] > 0)
    place_geometry(near_ref, 1, 2, after_ref, second_ref[0], spot_ref[0] < GX - 1)
    weigh(second_ref[0], counts_ref, near_ref, mine_ref, (weight_a, weight_c), old_sums_ref, sums_ref)
    row_sums(sums_ref, diagonal_ref)
    live = live_ref[...]
    sums = jnp.where(live == 0.0, 0.0, diagonal_ref[...])
    inverse_ref[...] = live / (dirichlet_ref[...] + sums)
    diagonal_ref[...] = live * dirichlet_ref[...] + sums
    copies[0].wait()


def coarse_lift(values_ref, coarse_ref, basis_ref, part_ref):
    total = jnp.zeros((64, SLOTS), jnp.float32)
    for t in range(128):
        total = total + coarse_ref[:, t * SLOTS : (t + 1) * SLOTS] * values_ref[t : t + 1, :]
    part_ref[...] = jnp.broadcast_to(jnp.sum(total, axis=1, keepdims=True), (64, SLOTS))
    sums = [[jnp.zeros((8, SLOTS), jnp.float32) for _ in range(2)] for _ in range(2)]
    for k in range(64):
        scale = jnp.broadcast_to(part_ref[k : k + 1, :], (8, SLOTS))
        for y in range(2):
            sums[k % 2][y] = sums[k % 2][y] + scale * basis_ref[k, y]
    return jnp.stack([sums[0][y] + sums[1][y] for y in range(2)])


def total_of(gathered_ref, at):
    rows = gathered_ref[pl.ds(1, 128, stride=2), :]
    lane = lax.broadcasted_iota(jnp.int32, rows.shape, 1)
    return jnp.sum(jnp.where(lane == at, rows, 0.0))


def first_smooth_kernel(
    second_ref, gathered_ref, coarse_ref, basis_ref, live_ref, residual_ref, inverse_ref,
    smoothed_ref, face_ref, part_ref,
):
    lifted = coarse_lift(gathered_ref, coarse_ref, basis_ref, part_ref)
    smoothed = residual_ref[...] * inverse_ref[...] + live_ref[...] * lifted
    smoothed_ref[...] = smoothed
    put_face(face_ref, smoothed, second_ref[0])


def second_smooth_kernel(
    second_ref, gathered_ref, coefficient_ref, coarse_ref, basis_ref, live_ref, residual_ref, inverse_ref,
    smoothed_ref, image_ref, new_coefficient_ref, new_residual_ref, new_smoothed_ref, face_ref, part_ref,
):
    step = total_of(gathered_ref, 0) / total_of(gathered_ref, 1)
    new_coefficient_ref[...] = coefficient_ref[...] - step * gathered_ref[pl.ds(0, 128, stride=2), :]
    lifted = coarse_lift(new_coefficient_ref, coarse_ref, basis_ref, part_ref)
    residual = residual_ref[...] - step * image_ref[...]
    new_residual_ref[...] = residual
    smoothed = residual * inverse_ref[...] + live_ref[...] * lifted
    new_smoothed_ref[...] = smoothed
    put_face(face_ref, smoothed, second_ref[0])


def third_smooth_kernel(
    gathered_ref, before_ref, coefficient_ref, coarse_ref, basis_ref, live_ref, residual_ref, inverse_ref,
    first_ref, first_image_ref, smoothed_ref, image_ref,
    pressure_ref, new_residual_ref, new_smoothed_ref, direction_ref, payload_ref, values_ref, part_ref,
):
    inner_first, curve_first = total_of(before_ref, 0), total_of(before_ref, 1)
    inner, curve = total_of(gathered_ref, 0), total_of(gathered_ref, 1)
    cross = total_of(gathered_ref, 2) + total_of(gathered_ref, 3)
    step_first = inner_first / curve_first
    ratio = inner / inner_first
    step = inner / (curve + ratio * (cross + ratio * curve_first))
    values_ref[...] = coefficient_ref[...] - step * (
        gathered_ref[pl.ds(0, 128, stride=2), :] + ratio * before_ref[pl.ds(0, 128, stride=2), :]
    )
    lifted = coarse_lift(values_ref, coarse_ref, basis_ref, part_ref)
    direction = smoothed_ref[...] + ratio * first_ref[...]
    direction_ref[...] = direction
    pressure_ref[...] = step_first * first_ref[...] + step * direction
    residual = residual_ref[...] - step * (image_ref[...] + ratio * first_image_ref[...])
    new_residual_ref[...] = residual
    smoothed = residual * inverse_ref[...] + live_ref[...] * lifted
    new_smoothed_ref[...] = smoothed
    payload_ref[...] = inner_row([(residual, smoothed), (residual_ref[...], smoothed_ref[...])])


def place_field(near_ref, slab, block_ref, second):
    def put(y, z, row):
        near_ref[slab, y, z] = jnp.broadcast_to(row, (8, SLOTS))

    assemble(lambda at: block_ref[at], second, put)


def apply_weights(second, counts_ref, near_ref, weight_refs, old_sums_ref, sums_ref):
    def one_cell(y, z, layer, layers):
        cell = y * 8 + z
        groups = (counts_ref[0, y, z] + 7) >> 3

        def some_groups(first, count):
            spots = [pl.ds(pl.multiple_of((first + g) * 8, 8), 8) for g in range(count)]
            parts = [[jnp.zeros((8, SLOTS), jnp.float32) for _ in range(3)] for _ in range(count)]
            if old_sums_ref is not None:
                for g in range(count):
                    parts[g][0] = old_sums_ref[cell, spots[g], :]
            for slab, weight_ref in enumerate(weight_refs):
                for b, c in [(b, layer + c) for b in range(3) for c in range(layers)]:
                    near = near_ref[slab, y + b, z + c]
                    for g in range(count):
                        parts[g][b] = parts[g][b] + weight_ref[cell, first + g, b * 3 + c] * near
            for g in range(count):
                sums_ref[cell, spots[g], :] = parts[g][0] + parts[g][1] + parts[g][2]

        def four_groups(quad, _):
            some_groups(quad * 4, 4)
            return 0

        def two_groups(pair, _):
            some_groups((groups >> 2) * 4 + pair * 2, 2)
            return 0

        lax.fori_loop(0, groups >> 2, four_groups, 0)
        lax.fori_loop(0, ((groups & 3) + 1) >> 1, two_groups, 0)

    each_cell(second, one_cell)


def middle_image_kernel(second_ref, counts_ref, weight_ref, block_ref, sums_ref, near_ref):
    place_field(near_ref, 0, block_ref, second_ref[0])
    apply_weights(second_ref[0], counts_ref, near_ref, (weight_ref,), None, sums_ref)


def image_kernel(
    second_ref, counts_ref, weight_a, weight_c, own_ref, before_ref, after_ref, old_sums_ref,
    live_ref, diagonal_ref, residual_ref, basis_ref, *rest,
):
    olds, (image_ref, payload_ref, near_ref, sums_ref, part_ref) = rest[:-5], rest[-5:]
    second = second_ref[0]
    place_field(near_ref, 0, before_ref, second)
    place_field(near_ref, 1, after_ref, second)
    apply_weights(second_ref[0], counts_ref, near_ref, (weight_a, weight_c), old_sums_ref, sums_ref)
    row_sums(sums_ref, image_ref)
    own = own_ref[...]
    image = jnp.where(live_ref[...] == 0.0, 0.0, diagonal_ref[...] * own - image_ref[...])
    image_ref[...] = image
    payload_ref[0:1, :] = project(basis_ref, image, part_ref, second)
    pairs = [(residual_ref[...], own), (own, image)]
    if olds:
        first_ref, first_image_ref = olds
        pairs += [(own, first_image_ref[...]), (first_ref[...], image)]
    payload_ref[1:2, :] = inner_row(pairs)


def swap(x):
    return lax.ppermute(x, "gz", [(0, 1), (1, 0)])


def turns(axis):
    size = lax.axis_size(axis)
    up = [(i, (i + 1) % size) for i in range(size)]
    return up, [(j, i) for i, j in up]


def around(field, gy_spot, across):
    count = field.shape[0]
    side = f32(count, 2, 8, SLOTS)
    upper, lower = call(side_faces_kernel, (side, side), [VM] * 2)(field, across)
    up, down = turns("gy")
    below = lax.ppermute(upper, "gy", up)
    above = lax.ppermute(lower, "gy", down)
    block = call(block_kernel, f32(count, 5, 8, SLOTS), [SM] + [VM] * 4)(gy_spot, field, across, below, above)
    up, down = turns("gx")
    return block, lax.ppermute(block, "gx", up), lax.ppermute(block, "gx", down)


def gather(payload, theirs=None, rows=None):
    theirs = swap(payload) if theirs is None else theirs
    rows = payload.shape[0] if rows is None else rows
    spread = call(spread_kernel, f32(128, rows, SLOTS), [VM] * 2)(payload, theirs)
    got = lax.all_to_all(spread, ("gx", "gy"), 0, 0, tiled=True)
    return got.reshape(128 * rows, SLOTS)


def per_device(offsets, counts, correction, dirichlet, right_side, deflation, coarse_inverse):
    second = lax.axis_index("gz").astype(jnp.int32)
    second = second.reshape(1)
    gx_spot, gy_spot = (lax.axis_index(axis).astype(jnp.int32).reshape(1) for axis in ("gx", "gy"))
    block = lambda x: x.reshape(2, 8, SLOTS)
    offsets = offsets.reshape(3, 2, 8, SLOTS)
    dirichlet, right_side, correction = block(dirichlet), block(right_side), block(correction)
    basis = deflation.reshape(64, 2, 8, SLOTS)
    cells = f32(2, 8, SLOTS)

    onchip = lambda x: pltpu.with_memory_space_constraint(x, pltpu.VMEM)
    outside = lambda x: pltpu.with_memory_space_constraint(x, pltpu.HBM)
    vmem = lambda *shape: pltpu.VMEM(shape, jnp.float32)
    part = vmem(64, SLOTS)

    geometry, live, residual, packed, counts, dirichlet, basis = call(
        prepare_kernel,
        (
            f32(4, 2, 8, SLOTS), cells, cells, f32(16, SLOTS),
            pltpu.VMEM((1, 2, 8), jnp.int32), vmem(2, 8, SLOTS), vmem(64, 2, 8, SLOTS),
        ),
        [SM] + [ANY] * 6,
        [
            pltpu.SMEM((1, 2, 8), jnp.int32), vmem(3, 2, 8, SLOTS), vmem(2, 8, SLOTS), vmem(2, 8, SLOTS), part,
            pltpu.SemaphoreType.DMA((7,)),
        ],
    )(second, *map(outside, (counts, offsets, correction, right_side, dirichlet, basis)))
    counts, dirichlet, basis = onchip(counts), onchip(dirichlet), onchip(basis)
    theirs = swap(packed)
    coefficient = gather(packed, theirs, 1)
    block, before, after = around(geometry, gy_spot, theirs)
    coefficient, block, centre = lax.optimization_barrier((coefficient, block, geometry))
    mine = call(centre_kernel, f32(16, 4, SLOTS, SLOTS), [VM])(centre)

    sums_shape = f32(16, SLOTS, SLOTS)
    weight_shape = vmem(16, 16, 9, 8, SLOTS)
    weight_b, sums = call(
        middle_weights_kernel,
        (weight_shape, sums_shape),
        [SM, SM] + [VM] * 2,
        [vmem(4, 1, 4, 10, 8, SLOTS)],
    )(second, counts, mine, block)
    weight_a, weight_c, diagonal, inverse, coarse = call(
        outer_weights_kernel,
        (weight_shape, weight_shape, cells, cells, vmem(64, 128 * SLOTS)),
        [SM, SM, SM] + [VM] * 6 + [ANY],
        [vmem(4, 2, 4, 10, 8, SLOTS), vmem(16, SLOTS, SLOTS), pltpu.SemaphoreType.DMA((1,))],
    )(second, gx_spot, counts, before, after, sums, mine, live, dirichlet, outside(coarse_inverse))
    weight_a, weight_b, weight_c, coarse = map(onchip, (weight_a, weight_b, weight_c, coarse))

    def image_of(field, face, residual, *olds):
        block, before, after = (piece[0] for piece in around(field[None], gy_spot, swap(face)))
        sums = call(middle_image_kernel, sums_shape, [SM, SM] + [VM] * 2, [vmem(1, 4, 10, 8, SLOTS)])(
            second, counts, weight_b, block
        )
        return call(
            image_kernel,
            (cells, f32(2, SLOTS)),
            [SM, SM] + [VM] * (10 + len(olds)),
            [vmem(2, 4, 10, 8, SLOTS), vmem(16, SLOTS, SLOTS), part],
        )(
            second, counts, weight_a, weight_c, field, before, after, sums,
            live, diagonal, residual, basis, *olds,
        )

    face_shape = f32(1, 2, SLOTS)
    smoothed, face = call(first_smooth_kernel, (cells, face_shape), [SM] + [VM] * 6, [part])(
        second, coefficient, coarse, basis, live, residual, inverse
    )
    image, payload = image_of(smoothed, face, residual)
    gathered_first = gather(payload)
    coefficient, residual, second_smoothed, face = call(
        second_smooth_kernel, (f32(128, SLOTS), cells, cells, face_shape), [SM] + [VM] * 9, [part]
    )(second, gathered_first, coefficient, coarse, basis, live, residual, inverse, smoothed, image)
    second_image, payload = image_of(second_smoothed, face, residual, smoothed, image)
    gathered = gather(payload)
    pressure, residual, third_smoothed, direction, payload = call(
        third_smooth_kernel,
        (vmem(2, 8, SLOTS), vmem(2, 8, SLOTS), cells, cells, f32(1, SLOTS)),
        [VM] * 12,
        [pltpu.VMEM((128, SLOTS), jnp.float32), part],
    )(
        gathered, gathered_first, coefficient, coarse, basis, live, residual, inverse,
        smoothed, image, second_smoothed, second_image,
    )
    pressure, residual, direction = call(finish_kernel, (cells, cells, cells), [VM] * 5)(
        gather(payload), third_smoothed, direction, onchip(pressure), onchip(residual)
    )
    shape = (1, 2, 8, SLOTS)
    return pressure.reshape(shape), residual.reshape(shape), direction.reshape(shape)


def solution(mesh):
    field = P("gx", "gy", "gz", None)
    in_specs = (
        P(None, "gx", "gy", "gz", None),
        P("gx", "gy", "gz"),
        field,
        field,
        field,
        P(None, "gx", "gy", "gz", None),
        P(("gx", "gy", "gz"), None),
    )
    return jax.shard_map(per_device, mesh=mesh, in_specs=in_specs, out_specs=(field,) * 3, check_vma=False)
```
